128 devices in a mesh: gy: 8 (over z, core), gx: 16 (over y, x).
Axes of the slice: x: 4, y: 4, z: 4, core: 2. Of those that a mesh axis runs over, the one named last changes fastest.
Arguments:
- radiance: bfloat16 [512, 512, 4096], P('gy', 'gx'), may hold values from -64 to 64
- kernel: float32 [3, 3, 4096], replicated, may hold values from 0.05 to 0.5
- test_matrix: bfloat16 [4096, 128], replicated, may hold values from -0.09375 to 0.09375
Outputs:
- basis_out: float32 [512, 512, 128], P('gy', 'gx')
- coeffs: float32 [128, 4096], replicated
The draws below stay inside these ranges and needn't reach their ends.
All inputs are finite; a program needn't handle non-finite values.
Results may differ from the reference program's by a relative error of at most 0.00085.
The reference program's roundings to bfloat16 on the way count: a program that leaves them out, or rounds other values in their place, can miss the bound.
Values may be sent and summed in bfloat16 or wider, within the bound.
No kernel may reach another device: no remote copies, remote signals or barrier semaphores. Data moves between devices by JAX's collectives and lax.ppermute only.
A program may use at most 192 MiB of HBM per device.

```python
import math
import jax
import jax.numpy as jnp
from jax import lax

C = 4096
K = 128
TH = 64
H = 512
W = 512
PIXELS = 262144
N_GY = 8


def draw_radiance(key, part):
    key_factor, key_pixel, key_noise = jax.random.split(key, 3)
    channel_factor = jax.random.randint(key_factor, (K, C), -2, 3).astype(jnp.float32)
    octave = (jnp.arange(K, dtype=jnp.int32) * 8 // K).astype(jnp.float32)
    strength = jnp.exp2(-octave - 5.0)
    column_place = jnp.arange(W, dtype=jnp.float32) / W

    def one_row(row_index):
        pixel_factor = jax.random.randint(jax.random.fold_in(key_pixel, row_index), (W, K), -2, 3).astype(jnp.float32)
        low_rank = jnp.dot(pixel_factor * strength, channel_factor, precision=lax.Precision.HIGHEST)
        noise_key = jax.random.fold_in(key_noise, row_index)
        row_place = row_index.astype(jnp.float32) / H
        noise = jax.random.truncated_normal(noise_key, -4.0, 4.0, (W, C), jnp.float32)
        brightness = jnp.exp2(1.5 * (row_place + column_place))
        return ((low_rank + noise) * brightness[:, None]).astype(jnp.bfloat16)
    return lax.map(one_row, jnp.arange(H, dtype=jnp.int32))


def centred(stream_key, extent, scale, bound, kind=jnp.bfloat16):
    result = jax.random.normal(stream_key, extent, jnp.float32) * scale
    return jnp.minimum(jnp.maximum(result, -bound), bound).astype(kind)


def setup_inputs(seed: int = 0) -> dict:
    key_of = jax.random.split(jax.random.key(seed), 4)
    radiance = draw_radiance(jax.random.fold_in(key_of[3], 71), 0)
    kernel = jnp.clip(jnp.exp(jax.random.uniform(key_of[1], (3, 3, C), jnp.float32, math.log(0.05), math.log(0.5))), 0.05, 0.5)
    test_matrix = centred(key_of[2], (C, K), C ** -0.5, 0.09375)
    return dict(radiance=radiance, kernel=kernel, test_matrix=test_matrix)


def smooth_block(padded, kernel, row_total, col_total):
    summed = jnp.zeros((row_total, col_total, padded.shape[2]), jnp.float32)
    for row_shift in range(3):
        for col_shift in range(3):
            window = padded[row_shift:row_shift + row_total, col_shift:col_shift + col_total].astype(jnp.float32)
            summed = summed + kernel[row_shift, col_shift] * window
    return summed.astype(jnp.bfloat16)

def factor_basis(values):
    gram_all = jnp.dot(values.T.astype(jnp.float32), values.astype(jnp.float32), precision=lax.Precision.HIGHEST, preferred_element_type=jnp.float32)
    triangle = jnp.linalg.cholesky(gram_all)
    return lax.linalg.triangular_solve(triangle, values, left_side=False, lower=True, transpose_a=True)

def reference(radiance, kernel, test_matrix):
    zero_row = jnp.zeros((1, W, C), radiance.dtype)

    def one_block(block_index):
        row_start = block_index * TH
        upper_rim = lax.dynamic_slice_in_dim(radiance, jnp.maximum(row_start - 1, 0).astype(jnp.int32), 1, 0)
        lower_rim = lax.dynamic_slice_in_dim(radiance, jnp.minimum(row_start + TH, H - 1).astype(jnp.int32), 1, 0)
        upper_rim = jnp.where(block_index > 0, upper_rim, zero_row)
        lower_rim = jnp.where(block_index < N_GY - 1, lower_rim, zero_row)
        middle = lax.dynamic_slice_in_dim(radiance, row_start.astype(jnp.int32), TH, 0)
        stacked = jnp.concatenate([upper_rim, middle, lower_rim], 0)
        padded = jnp.pad(stacked, ((0, 0), (1, 1), (0, 0)))
        return smooth_block(padded, kernel, TH, W)
    blocks = lax.map(one_block, jnp.arange(N_GY, dtype=jnp.int32))
    flattened = blocks.reshape(H * W, C)
    sketch = jnp.dot(flattened.astype(jnp.float32), test_matrix.astype(jnp.float32), preferred_element_type=jnp.float32)
    first_basis = factor_basis(sketch).astype(jnp.bfloat16)
    range_map = jnp.dot(first_basis.T.astype(jnp.float32), flattened.astype(jnp.float32), preferred_element_type=jnp.float32).astype(jnp.bfloat16)
    second = jnp.dot(flattened.astype(jnp.float32), range_map.T.astype(jnp.float32), preferred_element_type=jnp.float32)
    basis_out = factor_basis(second) * math.sqrt(PIXELS)
    basis_half = basis_out.astype(jnp.bfloat16)
    coeffs = jnp.dot(basis_half.T.astype(jnp.float32), flattened.astype(jnp.float32), preferred_element_type=jnp.float32) * (math.sqrt(C) / PIXELS)
    return (basis_out.reshape(H, W, K), coeffs)
```

```python
import math

import jax
import jax.numpy as jnp
from jax import lax
from jax.experimental import pallas as pl
from jax.experimental.pallas import tpu as pltpu
from jax.sharding import PartitionSpec as P

HIGH = lax.Precision.HIGHEST
BOTH = ("gy", "gx")


def xor_permute(value, axis, mask):
    return lax.ppermute(value, axis, [(i, i ^ mask) for i in range(lax.axis_size(axis))])


def shift_permute(value, axis, step):
    devices = lax.axis_size(axis)
    pairs = [(i, i + step) for i in range(devices) if 0 <= i + step < devices]
    return lax.ppermute(value, axis, pairs)


def params(mib, axes=0):
    return pltpu.CompilerParams(
        vmem_limit_bytes=mib << 20, dimension_semantics=("arbitrary",) * axes if axes else None
    )


def smooth_body(
    x_ref, top_ref, bot_ref, left_ref, right_ref, cl_ref, cr_ref, kern_ref, test_ref,
    flat_ref, sketch_ref, gram_ref, lt_ref, rt_ref,
):
    step, steps = pl.program_id(0), pl.num_programs(0)
    rows, cols, width = x_ref.shape
    f32 = jnp.float32

    def side(edge_ref, corner_ref, b):
        edge = edge_ref[...].astype(f32)
        corner = corner_ref[...].astype(f32)
        above = jnp.concatenate([corner[0:1], edge[:-1]], axis=0)
        below = jnp.concatenate([edge[1:], corner[1:2]], axis=0)
        taps = [kern_ref[3 * a + b : 3 * a + b + 1, :] for a in range(3)]
        return taps[0] * above + taps[1] * edge + taps[2] * below

    lt_ref[...] = side(left_ref, cl_ref, 0)
    rt_ref[...] = side(right_ref, cr_ref, 2)
    group = 8
    place = lax.broadcasted_iota(jnp.int32, (cols, 128), 0)
    for chunk in range(width // 128):
        lanes = slice(chunk * 128, chunk * 128 + 128)
        taps = [jnp.broadcast_to(kern_ref[i : i + 1, lanes], (cols, 128)) for i in range(9)]

        def body(g, carry, lanes=lanes, taps=taps):
            prev, here = carry
            start = pl.multiple_of(g * group, group)
            lefts = lt_ref[pl.ds(start, group), lanes]
            rights = rt_ref[pl.ds(start, group), lanes]
            for r in range(group):
                h = g * group + r
                if r == group - 1:
                    last = g == rows // group - 1
                    after = x_ref[jnp.minimum(h + 1, rows - 1), :, lanes]
                    after = jnp.where(last, bot_ref[:, lanes], after)
                else:
                    after = x_ref[h + 1, :, lanes]
                after = after.astype(f32)
                t = [taps[b] * prev + taps[3 + b] * here + taps[6 + b] * after for b in range(3)]
                left = jnp.where(place == 0, lefts[r : r + 1], pltpu.roll(t[0], 1, 0))
                right = jnp.where(
                    place == cols - 1, rights[r : r + 1], pltpu.roll(t[2], cols - 1, 0)
                )
                total = t[1] + left + right
                start = pl.multiple_of(h * cols, cols)
                flat_ref[pl.ds(start, cols), lanes] = total.astype(jnp.bfloat16)
                prev, here = here, after
            return prev, here

        first = (top_ref[:, lanes].astype(f32), x_ref[0, :, lanes].astype(f32))
        lax.fori_loop(0, rows // group, body, first)

    part = jnp.dot(flat_ref[...], test_ref[...], preferred_element_type=f32)

    @pl.when(step == 0)
    def _():
        sketch_ref[...] = part

    @pl.when(step > 0)
    def _():
        sketch_ref[...] += part

    @pl.when(step == steps - 1)
    def _():
        values = sketch_ref[...]
        gram_ref[...] = lax.dot_general(
            values, values, (((0,), (0,)), ((), ())), precision=HIGH, preferred_element_type=f32
        )


def smooth_sketch(x, halos, kernel, test_matrix):
    rows, cols, channels = x.shape
    k = test_matrix.shape[1]
    width = 512
    edge = lambda n: pl.BlockSpec((n, width), lambda j: (0, j))
    return pl.pallas_call(
        smooth_body,
        grid=(channels // width,),
        in_specs=[
            pl.BlockSpec((rows, cols, width), lambda j: (0, 0, j)),
            edge(cols), edge(cols), edge(rows), edge(rows), edge(2), edge(2), edge(9),
            pl.BlockSpec((width, k), lambda j: (j, 0)),
        ],
        out_specs=[
            pl.BlockSpec((rows * cols, width), lambda j: (0, j)),
            pl.BlockSpec((rows * cols, k), lambda j: (0, 0)),
            pl.BlockSpec((k, k), lambda j: (0, 0)),
        ],
        out_shape=[
            jax.ShapeDtypeStruct((rows * cols, channels), jnp.bfloat16),
            jax.ShapeDtypeStruct((rows * cols, k), jnp.float32),
            jax.ShapeDtypeStruct((k, k), jnp.float32),
        ],
        scratch_shapes=[pltpu.VMEM((rows, width), jnp.float32)] * 2,
        compiler_params=params(40, 1),
        name="smooth_sketch",
    )(x, *halos, kernel.reshape(9, channels), test_matrix)


def inverse_factor(gram, work_ref):
    n = gram.shape[0]
    f32 = jnp.float32
    row_id = lax.broadcasted_iota(jnp.int32, (n, n), 0)
    col_id = lax.broadcasted_iota(jnp.int32, (n, n), 1)
    work_ref[:, :n] = gram
    work_ref[:, n:] = (row_id == col_id).astype(f32)
    sub = lax.broadcasted_iota(jnp.int32, (8, 2 * n), 0)
    sub1 = lax.broadcasted_iota(jnp.int32, (8, 1), 0)
    for p in range(n // 8):
        panel = work_ref[8 * p : 8 * p + 8, :]
        for i in range(8):
            c = 8 * p + i
            column = panel[:, c : c + 1]
            scale = lax.rsqrt(column[i : i + 1])
            row = panel[i : i + 1, :] * scale
            factor = jnp.where(sub1 > i, column * scale, 0.0)
            panel = jnp.where(sub == i, row, panel - factor * row)
        work_ref[8 * p : 8 * p + 8, :] = panel
        rest = 8 * p + 8
        if rest < n:
            update = lax.dot_general(
                panel[:, :n], panel, (((0,), (0,)), ((), ())),
                precision=HIGH, preferred_element_type=f32,
            )
            work_ref[rest:, :] -= update[rest:, :]
    return jnp.where(row_id >= col_id, work_ref[:, n:], 0.0)


def times_transposed(values, matrix):
    return lax.dot_general(
        values, matrix, (((1,), (1,)), ((), ())), precision=HIGH,
        preferred_element_type=jnp.float32,
    )


def project_body(core_ref, gram_ref, sketch_ref, flat_ref, out_ref, work_ref, basis_ref):
    @pl.when(pl.program_id(0) == 0)
    def _():
        inverse = inverse_factor(gram_ref[...], work_ref)
        basis = times_transposed(sketch_ref[...], inverse)
        basis_ref[...] = basis.astype(jnp.bfloat16).T

    product = jnp.dot(basis_ref[...], flat_ref[...], preferred_element_type=jnp.float32)
    out_ref[0] = product.T


def project(core, gram, sketch, flat):
    pixels, channels = flat.shape
    k = gram.shape[0]
    width = 512
    half = channels // width // 2
    whole = lambda *shape: pl.BlockSpec(shape, lambda j, core: (0,) * len(shape))
    return pl.pallas_call(
        project_body,
        grid_spec=pltpu.PrefetchScalarGridSpec(
            num_scalar_prefetch=1,
            grid=(channels // width,),
            in_specs=[
                whole(k, k), whole(pixels, k),
                pl.BlockSpec((pixels, width), lambda j, core: (0, j)),
            ],
            out_specs=pl.BlockSpec(
                (1, width, k), lambda j, core: ((j // half) ^ core[0], j % half, 0)
            ),
            scratch_shapes=[
                pltpu.VMEM((k, 2 * k), jnp.float32), pltpu.VMEM((k, pixels), jnp.bfloat16),
            ],
        ),
        out_shape=jax.ShapeDtypeStruct((2, channels // 2, k), jnp.float32),
        compiler_params=params(40, 1),
        name="project",
    )(core, gram, sketch, flat)


def second_body(core_ref, flat_ref, range_ref, second_ref, out_ref, acc_ref):
    step, steps = pl.program_id(0), pl.num_programs(0)
    f32, bf16 = jnp.float32, jnp.bfloat16
    k = range_ref.shape[1]
    values = jnp.dot(flat_ref[...], range_ref[...], preferred_element_type=f32)
    second_ref[...] = values
    high = values.astype(bf16)
    low = (values - high.astype(f32)).astype(bf16)
    both = jnp.concatenate([high, low], axis=1).T

    @pl.when(step == 0)
    def _():
        acc_ref[...] = jnp.dot(both, flat_ref[...], preferred_element_type=f32)

    @pl.when(step > 0)
    def _():
        acc_ref[...] += jnp.dot(both, flat_ref[...], preferred_element_type=f32)

    @pl.when(step == steps - 1)
    def _():
        half = out_ref.shape[1]
        for part in range(2):
            lanes = slice(part * half, part * half + half)
            out_ref[part ^ core_ref[0]] = (acc_ref[:k, lanes] + acc_ref[k:, lanes]).T


def second_step(core, flat, range_map):
    pixels, channels = flat.shape
    k = range_map.shape[1]
    height = 512
    return pl.pallas_call(
        second_body,
        grid_spec=pltpu.PrefetchScalarGridSpec(
            num_scalar_prefetch=1,
            grid=(pixels // height,),
            in_specs=[
                pl.BlockSpec((height, channels), lambda i, core: (i, 0)),
                pl.BlockSpec((channels, k), lambda i, core: (0, 0)),
            ],
            out_specs=[
                pl.BlockSpec((height, k), lambda i, core: (i, 0)),
                pl.BlockSpec((2, channels // 2, k), lambda i, core: (0, 0, 0)),
            ],
            scratch_shapes=[pltpu.VMEM((2 * k, channels), jnp.float32)],
        ),
        out_shape=[
            jax.ShapeDtypeStruct((pixels, k), jnp.float32),
            jax.ShapeDtypeStruct((2, channels // 2, k), jnp.float32),
        ],
        compiler_params=params(44, 1),
        name="second_step",
    )(core, flat, range_map)


def finish_body(basis_scale, coeff_scale, range_ref, moment_ref, second_ref, basis_ref, coeffs_ref, work_ref):
    moment = moment_ref[...]
    gram = lax.dot_general(
        range_ref[...].astype(jnp.float32), moment, (((0,), (0,)), ((), ())), precision=HIGH,
        preferred_element_type=jnp.float32,
    )
    inverse = inverse_factor(gram, work_ref)
    basis_ref[...] = times_transposed(second_ref[...], inverse) * basis_scale
    coeffs_ref[...] = times_transposed(inverse, moment) * coeff_scale


def finish(range_map, moment, second, basis_scale, coeff_scale):
    channels, k = moment.shape

    def body(*refs):
        finish_body(basis_scale, coeff_scale, *refs)

    return pl.pallas_call(
        body,
        out_shape=[
            jax.ShapeDtypeStruct(second.shape, jnp.float32),
            jax.ShapeDtypeStruct((k, channels), jnp.float32),
        ],
        scratch_shapes=[pltpu.VMEM((k, 2 * k), jnp.float32)],
        compiler_params=params(40),
        name="finish",
    )(range_map, moment, second)


def all_sum(pair, core, dtype):
    gy, gx = lax.axis_size("gy"), lax.axis_size("gx")
    groups = [[y * gx + x for y in range(c, gy, 2) for x in range(gx)] for c in range(2)]
    half, k = pair.shape[1:]
    members = gy * gx // 2
    swap = lambda v: lax.all_to_all(v, BOTH, 0, 0, axis_index_groups=groups, tiled=True)
    mine = pair[0] + xor_permute(pair[1], "gy", 1)
    parts = swap(mine.reshape(members, half // members, k))
    chunk = jnp.sum(parts, axis=0).astype(dtype)
    chunk = lax.optimization_barrier(chunk)
    whole = swap(jnp.broadcast_to(chunk[None], (members,) + chunk.shape)).reshape(half, k)
    other = xor_permute(whole, "gy", 1)
    first, last = jnp.where(core == 0, whole, other), jnp.where(core == 0, other, whole)
    return jnp.concatenate([first, last], axis=0)


def on_device(radiance, kernel, test_matrix):
    height, breadth, channels = radiance.shape
    devices = lax.axis_size("gy") * lax.axis_size("gx")
    pixel_count = height * breadth * devices
    core = lax.axis_index("gy") % 2
    core_arg = core.astype(jnp.int32).reshape(1)

    top = shift_permute(radiance[-1], "gy", 1)
    bottom = shift_permute(radiance[0], "gy", -1)
    left = shift_permute(radiance[:, -1], "gx", 1)
    right = shift_permute(radiance[:, 0], "gx", -1)
    rims = jnp.stack([top, bottom])
    left_ends = shift_permute(rims[:, -1], "gx", 1)
    right_ends = shift_permute(rims[:, 0], "gx", -1)
    halos = (top, bottom, left, right, left_ends, right_ends)

    flat, sketch, gram = smooth_sketch(radiance, halos, kernel, test_matrix)
    for axis, mask in (("gy", 1), ("gx", 1), ("gx", 3), ("gx", 4), ("gx", 12), ("gy", 2), ("gy", 6)):
        gram = gram + xor_permute(gram, axis, mask)
    range_map = all_sum(project(core_arg, gram, sketch, flat), core, jnp.bfloat16)
    second, pair = second_step(core_arg, flat, range_map)
    moment = all_sum(pair, core, jnp.float32)
    scale = math.sqrt(pixel_count)
    basis_out, coeffs = finish(
        range_map, moment, second, scale, scale * math.sqrt(channels) / pixel_count
    )
    return (basis_out.reshape(height, breadth, basis_out.shape[1]), coeffs)


def solution(mesh):
    placed = (P("gy", "gx", None), P(), P())
    return jax.shard_map(
        on_device, mesh=mesh, in_specs=placed, out_specs=(P("gy", "gx", None), P()), check_vma=False
    )
```

```python
import math

import jax
import jax.numpy as jnp
from jax import lax
from jax.experimental import pallas as pl
from jax.experimental.pallas import tpu as pltpu
from jax.sharding import PartitionSpec as P

HIGH = lax.Precision.HIGHEST
BOTH = ("gy", "gx")


def xor_permute(value, axis, mask):
    return lax.ppermute(value, axis, [(i, i ^ mask) for i in range(lax.axis_size(axis))])


def shift_permute(value, axis, step):
    devices = lax.axis_size(axis)
    pairs = [(i, i + step) for i in range(devices) if 0 <= i + step < devices]
    return lax.ppermute(value, axis, pairs)


def params(mib, axes=0):
    return pltpu.CompilerParams(
        vmem_limit_bytes=mib << 20, dimension_semantics=("arbitrary",) * axes if axes else None
    )


def smooth_body(
    core_ref, x_ref, top_ref, bot_ref, left_ref, right_ref, kern_ref, test_ref,
    flat_ref, sketch_ref, keep_ref, send_ref, lt_ref, rt_ref, pad_ref,
):
    step, steps = pl.program_id(0), pl.num_programs(0)
    rows, cols, width = x_ref.shape
    f32 = jnp.float32
    group = 8
    groups = rows // group

    def ordered(edge_ref):
        edge = edge_ref[...].astype(f32)
        spare = jnp.zeros((group - 2, width), f32)
        return jnp.concatenate(
            [edge[rows : rows + 1], edge[:rows], edge[rows + 1 : rows + 2], spare], axis=0
        )

    lt_ref[...] = ordered(left_ref)
    rt_ref[...] = ordered(right_ref)

    @pl.when(step == 0)
    def _():
        sketch_ref[...] = jnp.zeros_like(sketch_ref)

    def project_rows(g):
        span = pl.ds(pl.multiple_of(g * group * cols, group * cols), group * cols)
        return span, jnp.dot(flat_ref[span, :], test_ref[...], preferred_element_type=f32)

    def smooth_rows(g):
        base = pl.multiple_of(g * group, group)
        for chunk in range(width // 128):
            lanes = slice(chunk * 128, chunk * 128 + 128)
            pad = pad_ref.at[chunk % 2]
            taps = [
                [jnp.broadcast_to(kern_ref[a, b : b + 1, lanes], (cols, 128)) for b in range(3)]
                for a in range(3)
            ]
            lefts = lt_ref[pl.ds(base, 2 * group), lanes]
            rights = rt_ref[pl.ds(base, 2 * group), lanes]

            def fetch(q):
                if q == 0:
                    above = x_ref[jnp.maximum(base - 1, 0), :, lanes]
                    row = jnp.where(g == 0, top_ref[:, lanes], above)
                elif q == group + 1:
                    below = x_ref[jnp.minimum(base + group, rows - 1), :, lanes]
                    row = jnp.where(g == groups - 1, bot_ref[:, lanes], below)
                else:
                    row = x_ref[base + q - 1, :, lanes]
                row = row.astype(f32)
                at = q * (cols + 16) + 8
                pad[at - 1 : at, :] = lefts[q : q + 1]
                pad[at : at + cols, :] = row
                pad[at + cols : at + cols + 1, :] = rights[q : q + 1]
                return [pad[at - 1 : at - 1 + cols, :], row, pad[at + 1 : at + 1 + cols, :]]

            near = [fetch(0), fetch(1)]
            for r in range(group):
                near = near[-2:] + [fetch(r + 2)]
                total = None
                for a in range(3):
                    for b in range(3):
                        term = taps[a][b] * near[a][b]
                        total = term if total is None else total + term
                start = pl.multiple_of((base + r) * cols, cols)
                flat_ref[pl.ds(start, cols), lanes] = total.astype(jnp.bfloat16)

    def body(g, carry):
        span, part = project_rows(g - 1)
        smooth_rows(g)
        sketch_ref[span, :] += part
        return carry

    smooth_rows(0)
    lax.fori_loop(1, groups, body, 0)
    span, part = project_rows(groups - 1)
    sketch_ref[span, :] += part

    @pl.when(step == steps - 1)
    def _():
        values = sketch_ref[...]
        gram = lax.dot_general(
            values, values, (((0,), (0,)), ((), ())), precision=HIGH, preferred_element_type=f32
        )
        half = keep_ref.shape[0]

        @pl.when(core_ref[0] == 0)
        def _():
            keep_ref[...] = gram[:half]
            send_ref[...] = gram[half:]

        @pl.when(core_ref[0] == 1)
        def _():
            keep_ref[...] = gram[half:]
            send_ref[...] = gram[:half]


def smooth_sketch(core, x, halos, kernel, test_matrix):
    rows, cols, channels = x.shape
    k = test_matrix.shape[1]
    width = 512
    edge = lambda n: pl.BlockSpec((n, width), lambda j, core: (0, j))
    fixed = lambda n: pl.BlockSpec((n, k), lambda j, core: (0, 0))
    return pl.pallas_call(
        smooth_body,
        grid_spec=pltpu.PrefetchScalarGridSpec(
            num_scalar_prefetch=1,
            grid=(channels // width,),
            in_specs=[
                pl.BlockSpec((rows, cols, width), lambda j, core: (0, 0, j)),
                edge(cols), edge(cols), edge(rows + 8), edge(rows + 8),
                pl.BlockSpec((3, 3, width), lambda j, core: (0, 0, j)),
                pl.BlockSpec((width, k), lambda j, core: (j, 0)),
            ],
            out_specs=[edge(rows * cols), fixed(rows * cols), fixed(k // 2), fixed(k // 2)],
            scratch_shapes=[pltpu.VMEM((rows + 8, width), jnp.float32)] * 2
            + [pltpu.VMEM((2, 10 * (cols + 16), 128), jnp.float32)],
        ),
        out_shape=[
            jax.ShapeDtypeStruct((rows * cols, channels), jnp.bfloat16),
            jax.ShapeDtypeStruct((rows * cols, k), jnp.float32),
            jax.ShapeDtypeStruct((k // 2, k), jnp.float32),
            jax.ShapeDtypeStruct((k // 2, k), jnp.float32),
        ],
        compiler_params=params(40, 1),
        name="smooth_sketch",
    )(core, x, *halos, kernel, test_matrix)


def columns_body(x_ref, top_ref, bot_ref, first_ref, last_ref, low_ref, high_ref, sems):
    rows, cols, _ = x_ref.shape
    copies = [
        pltpu.make_async_copy(x_ref.at[:, pl.ds(0, 8), :], low_ref, sems.at[0]),
        pltpu.make_async_copy(x_ref.at[:, pl.ds(cols - 8, 8), :], high_ref, sems.at[1]),
    ]
    for copy in copies:
        copy.start()
    for copy, place, held_ref, out_ref in zip(
        copies, (0, cols - 1), (low_ref, high_ref), (first_ref, last_ref)
    ):
        copy.wait()
        for lane in range(0, out_ref.shape[1], 512):
            lanes = slice(lane, lane + 512)
            column = held_ref[:, :, lanes].astype(jnp.float32)[:, place % 8]
            ends = [r[:, lanes].astype(jnp.float32)[place : place + 1] for r in (top_ref, bot_ref)]
            spare = jnp.zeros((6, 512), jnp.float32)
            joined = jnp.concatenate([column] + ends + [spare], axis=0)
            out_ref[:, lanes] = joined.astype(jnp.bfloat16)


def edge_columns(x, top, bottom):
    rows, cols, channels = x.shape
    return pl.pallas_call(
        columns_body,
        in_specs=[pl.BlockSpec(memory_space=pltpu.HBM)]
        + [pl.BlockSpec(memory_space=pltpu.VMEM)] * 2,
        out_shape=[jax.ShapeDtypeStruct((rows + 8, channels), x.dtype)] * 2,
        scratch_shapes=[pltpu.VMEM((rows, 8, channels), x.dtype)] * 2
        + [pltpu.SemaphoreType.DMA((2,))],
        compiler_params=params(20),
        name="edge_columns",
    )(x, top, bottom)


def factor_block(panel, low, sub, lane):
    shape = panel.shape
    d = [
        [jnp.broadcast_to(panel[i : i + 1, low + j : low + j + 1], shape) for j in range(i + 1)]
        for i in range(8)
    ]
    e = [[None] * 8 for _ in range(8)]
    for j in range(8):
        scale = lax.rsqrt(d[j][j])
        column = [d[i][j] * scale if i > j else None for i in range(8)]
        for k in range(j):
            e[j][k] = e[j][k] * scale
        e[j][j] = scale
        for i in range(j + 1, 8):
            for k in range(j + 1, i + 1):
                d[i][k] = d[i][k] - column[i] * column[k]
            for k in range(j):
                e[i][k] = e[i][k] - column[i] * e[j][k]
            e[i][j] = -column[i] * scale
    unit = jnp.where(lane == sub + low, 1.0, 0.0)
    panel = jnp.where((lane >= low) & (lane < low + 8), unit, panel)
    total = None
    for k in range(8):
        column = jnp.where(sub == k, e[k][k], 0.0)
        for i in range(k + 1, 8):
            column = jnp.where(sub == i, e[i][k], column)
        term = column * jnp.broadcast_to(panel[k : k + 1, :], shape)
        total = term if total is None else total + term
    return total


def inverse_factor(work_ref):
    n = work_ref.shape[0]
    row_id = lax.broadcasted_iota(jnp.int32, (n, n), 0)
    col_id = lax.broadcasted_iota(jnp.int32, (n, n), 1)
    sub = lax.broadcasted_iota(jnp.int32, (8, n), 0)
    lane = lax.broadcasted_iota(jnp.int32, (8, n), 1)
    panel = work_ref[0:8, :]
    for low in range(0, n, 8):
        near, far = low + 8, low + 16
        done = factor_block(panel, low, sub, lane)
        work_ref[low:near, :] = done
        if far < n:
            update = lax.dot_general(
                done, done, (((0,), (0,)), ((), ())), precision=HIGH,
                preferred_element_type=jnp.float32,
            )
            keep = (col_id[far:] < low) | (col_id[far:] >= near)
            rest = jnp.where(keep, work_ref[far:, :], 0.0) - update[far:, :]
        if near < n:
            turned = done.T[near:far, :]
            panel = jnp.where((lane < low) | (lane >= near), work_ref[near:far, :], 0.0)
            for k in range(8):
                panel = panel - jnp.broadcast_to(turned[:, k : k + 1], panel.shape) * (
                    jnp.broadcast_to(done[k : k + 1, :], panel.shape)
                )
        if far < n:
            work_ref[far:, :] = rest
    return jnp.where(row_id >= col_id, work_ref[...], 0.0)


def times_transposed(values, matrix):
    return lax.dot_general(
        values, matrix, (((1,), (1,)), ((), ())), precision=HIGH,
        preferred_element_type=jnp.float32,
    )


def project_body(
    core_ref, mine_ref, other_ref, sketch_ref, flat_ref, out_ref, work_ref, basis_ref
):
    @pl.when(pl.program_id(0) == 0)
    def _():
        half = mine_ref.shape[0]
        work_ref[pl.ds(pl.multiple_of(core_ref[0] * half, half), half), :] = mine_ref[...]
        work_ref[pl.ds(pl.multiple_of((1 - core_ref[0]) * half, half), half), :] = other_ref[...]
        inverse = inverse_factor(work_ref)
        basis = times_transposed(sketch_ref[...], inverse)
        basis_ref[...] = basis.astype(jnp.bfloat16).T

    product = jnp.dot(basis_ref[...], flat_ref[...], preferred_element_type=jnp.float32)
    out_ref[0] = product.T


def project(core, mine, other, sketch, flat):
    pixels, channels = flat.shape
    k = sketch.shape[1]
    width = 512
    half = channels // width // 2
    whole = lambda *shape: pl.BlockSpec(shape, lambda j, core: (0,) * len(shape))
    return pl.pallas_call(
        project_body,
        grid_spec=pltpu.PrefetchScalarGridSpec(
            num_scalar_prefetch=1,
            grid=(channels // width,),
            in_specs=[
                whole(k // 2, k), whole(k // 2, k), whole(pixels, k),
                pl.BlockSpec((pixels, width), lambda j, core: (0, j)),
            ],
            out_specs=pl.BlockSpec(
                (1, width, k), lambda j, core: ((j // half) ^ core[0], j % half, 0)
            ),
            scratch_shapes=[
                pltpu.VMEM((k, k), jnp.float32), pltpu.VMEM((k, pixels), jnp.bfloat16),
            ],
        ),
        out_shape=jax.ShapeDtypeStruct((2, channels // 2, k), jnp.float32),
        compiler_params=params(40, 1),
        name="project",
    )(core, mine, other, sketch, flat)


def second_body(core_ref, flat_ref, range_ref, second_ref, out_ref, acc_ref):
    step, steps = pl.program_id(0), pl.num_programs(0)
    f32, bf16 = jnp.float32, jnp.bfloat16
    k = range_ref.shape[1]
    values = jnp.dot(flat_ref[...], range_ref[...], preferred_element_type=f32)
    second_ref[...] = values
    high = values.astype(bf16)
    low = (values - high.astype(f32)).astype(bf16)
    both = jnp.concatenate([high, low], axis=1).T

    @pl.when(step == 0)
    def _():
        acc_ref[...] = jnp.dot(both, flat_ref[...], preferred_element_type=f32)

    @pl.when(step > 0)
    def _():
        acc_ref[...] += jnp.dot(both, flat_ref[...], preferred_element_type=f32)

    @pl.when(step == steps - 1)
    def _():
        half = out_ref.shape[1]
        for part in range(2):
            lanes = slice(part * half, part * half + half)
            out_ref[part ^ core_ref[0]] = (acc_ref[:k, lanes] + acc_ref[k:, lanes]).T


def second_step(core, flat, range_map):
    pixels, channels = flat.shape
    k = range_map.shape[1]
    height = 512
    return pl.pallas_call(
        second_body,
        grid_spec=pltpu.PrefetchScalarGridSpec(
            num_scalar_prefetch=1,
            grid=(pixels // height,),
            in_specs=[
                pl.BlockSpec((height, channels), lambda i, core: (i, 0)),
                pl.BlockSpec((channels, k), lambda i, core: (0, 0)),
            ],
            out_specs=[
                pl.BlockSpec((height, k), lambda i, core: (i, 0)),
                pl.BlockSpec((2, channels // 2, k), lambda i, core: (0, 0, 0)),
            ],
            scratch_shapes=[pltpu.VMEM((2 * k, channels), jnp.float32)],
        ),
        out_shape=[
            jax.ShapeDtypeStruct((pixels, k), jnp.float32),
            jax.ShapeDtypeStruct((2, channels // 2, k), jnp.float32),
        ],
        compiler_params=params(44, 1),
        name="second_step",
    )(core, flat, range_map)


def finish_body(basis_scale, coeff_scale, range_ref, moment_ref, second_ref, basis_ref, coeffs_ref, work_ref):
    moment = moment_ref[...]
    gram = lax.dot_general(
        range_ref[...].astype(jnp.float32), moment, (((0,), (0,)), ((), ())), precision=HIGH,
        preferred_element_type=jnp.float32,
    )
    work_ref[...] = gram
    inverse = inverse_factor(work_ref)
    basis_ref[...] = times_transposed(second_ref[...], inverse) * basis_scale
    coeffs_ref[...] = times_transposed(inverse, moment) * coeff_scale


def finish(range_map, moment, second, basis_scale, coeff_scale):
    channels, k = moment.shape

    def body(*refs):
        finish_body(basis_scale, coeff_scale, *refs)

    return pl.pallas_call(
        body,
        out_shape=[
            jax.ShapeDtypeStruct(second.shape, jnp.float32),
            jax.ShapeDtypeStruct((k, channels), jnp.float32),
        ],
        scratch_shapes=[pltpu.VMEM((k, k), jnp.float32)],
        compiler_params=params(40),
        name="finish",
    )(range_map, moment, second)


def all_sum(pair, core, dtype):
    gy, gx = lax.axis_size("gy"), lax.axis_size("gx")
    groups = [[y * gx + x for y in range(c, gy, 2) for x in range(gx)] for c in range(2)]
    half, k = pair.shape[1:]
    members = gy * gx // 2
    swap = lambda v: lax.all_to_all(v, BOTH, 0, 0, axis_index_groups=groups, tiled=True)
    mine = pair[0] + xor_permute(pair[1], "gy", 1)
    parts = swap(mine.reshape(members, half // members, k))
    chunk = jnp.sum(parts, axis=0).astype(dtype)
    chunk = lax.optimization_barrier(chunk)
    whole = swap(jnp.broadcast_to(chunk[None], (members,) + chunk.shape)).reshape(half, k)
    other = xor_permute(whole, "gy", 1)
    first, last = jnp.where(core == 0, whole, other), jnp.where(core == 0, other, whole)
    return jnp.concatenate([first, last], axis=0)


def on_device(radiance, kernel, test_matrix):
    height, breadth, channels = radiance.shape
    devices = lax.axis_size("gy") * lax.axis_size("gx")
    pixel_count = height * breadth * devices
    core = lax.axis_index("gy") % 2
    core_arg = core.astype(jnp.int32).reshape(1)

    top = shift_permute(radiance[-1], "gy", 1)
    bottom = shift_permute(radiance[0], "gy", -1)
    first, last = edge_columns(radiance, top, bottom)
    left = shift_permute(last, "gx", 1)
    right = shift_permute(first, "gx", -1)
    halos = (top, bottom, left, right)

    flat, sketch, mine, send = smooth_sketch(core_arg, radiance, halos, kernel, test_matrix)
    mine = mine + xor_permute(send, "gy", 1)
    for axis, mask in (("gx", 1), ("gx", 3), ("gx", 4), ("gx", 12), ("gy", 2), ("gy", 6)):
        mine = mine + xor_permute(mine, axis, mask)
    other = xor_permute(mine, "gy", 1)
    range_map = all_sum(project(core_arg, mine, other, sketch, flat), core, jnp.bfloat16)
    second, pair = second_step(core_arg, flat, range_map)
    moment = all_sum(pair, core, jnp.float32)
    scale = math.sqrt(pixel_count)
    basis_out, coeffs = finish(
        range_map, moment, second, scale, scale * math.sqrt(channels) / pixel_count
    )
    return (basis_out.reshape(height, breadth, basis_out.shape[1]), coeffs)


def solution(mesh):
    placed = (P("gy", "gx", None), P(), P())
    return jax.shard_map(
        on_device, mesh=mesh, in_specs=placed, out_specs=(P("gy", "gx", None), P()), check_vma=False
    )
```

```python
import math

import jax
import jax.numpy as jnp
from jax import lax
from jax.experimental import pallas as pl
from jax.experimental.pallas import tpu as pltpu
from jax.sharding import PartitionSpec as P

HIGH = lax.Precision.HIGHEST
BOTH = ("gy", "gx")
BORDER = 256


def xor_permute(value, axis, mask):
    return lax.ppermute(value, axis, [(i, i ^ mask) for i in range(lax.axis_size(axis))])


def shift_permute(value, axis, step):
    devices = lax.axis_size(axis)
    pairs = [(i, i + step) for i in range(devices) if 0 <= i + step < devices]
    return lax.ppermute(value, axis, pairs)


def params(mib, axes=0):
    return pltpu.CompilerParams(
        vmem_limit_bytes=mib << 20, dimension_semantics=("arbitrary",) * axes if axes else None
    )


def smooth_body(x_ref, kern_ref, test_ref, flat_ref, sketch_ref, gram_ref, pad_ref):
    step, steps = pl.program_id(0), pl.num_programs(0)
    rows, cols, width = x_ref.shape
    f32 = jnp.float32
    group = 8
    groups = rows // group
    sub = lax.broadcasted_iota(jnp.int32, (8, 128), 0)

    @pl.when(step == 0)
    def _():
        sketch_ref[...] = jnp.zeros_like(sketch_ref)

    def project_rows(g):
        span = pl.ds(pl.multiple_of(g * group * cols, group * cols), group * cols)
        return span, jnp.dot(flat_ref[span, :], test_ref[...], preferred_element_type=f32)

    def smooth_rows(g):
        base = pl.multiple_of(g * group, group)
        for chunk in range(width // 128):
            lanes = slice(chunk * 128, chunk * 128 + 128)
            pad = pad_ref.at[chunk % 2]
            taps = [
                [jnp.broadcast_to(kern_ref[a, b : b + 1, lanes], (cols, 128)) for b in range(3)]
                for a in range(3)
            ]

            def fetch(q):
                place = base + q - 1
                if q == 0:
                    place = jnp.maximum(place, 0)
                elif q == group + 1:
                    place = jnp.minimum(place, rows - 1)
                row = x_ref[place, :, lanes].astype(f32)
                at = q * (cols + 16) + 8
                pad[at : at + cols, :] = row
                return [pad[at - 1 : at - 1 + cols, :], row, pad[at + 1 : at + 1 + cols, :]]

            near = [fetch(0), fetch(1)]
            for r in range(group):
                near = near[-2:] + [fetch(r + 2)]
                total = None
                for a in range(3):
                    for b in range(3):
                        term = taps[a][b] * near[a][b]
                        total = term if total is None else total + term
                head = jnp.where(sub == 0, 0.0, total[:8])
                tail = jnp.where(sub == 7, 0.0, total[cols - 8 :])
                total = jnp.concatenate([head, total[8 : cols - 8], tail], axis=0)
                if r == 0:
                    total = jnp.where(g == 0, 0.0, total)
                if r == group - 1:
                    total = jnp.where(g == groups - 1, 0.0, total)
                start = pl.multiple_of((base + r) * cols, cols)
                flat_ref[pl.ds(start, cols), lanes] = total.astype(jnp.bfloat16)

    def body(g, carry):
        span, part = project_rows(g - 1)
        smooth_rows(g)
        sketch_ref[span, :] += part
        return carry

    smooth_rows(0)
    lax.fori_loop(1, groups, body, 0)
    span, part = project_rows(groups - 1)
    sketch_ref[span, :] += part

    @pl.when(step == steps - 1)
    def _():
        gram_ref[...] = gram_of(sketch_ref[...])


def gram_of(values):
    return lax.dot_general(
        values, values, (((0,), (0,)), ((), ())), precision=HIGH,
        preferred_element_type=jnp.float32,
    )


def smooth_sketch(x, kernel, test_matrix):
    rows, cols, channels = x.shape
    k = test_matrix.shape[1]
    width = 512
    total = rows * cols + BORDER
    fixed = lambda n: pl.BlockSpec((n, k), lambda j: (0, 0))
    return pl.pallas_call(
        smooth_body,
        grid=(channels // width,),
        in_specs=[
            pl.BlockSpec((rows, cols, width), lambda j: (0, 0, j)),
            pl.BlockSpec((3, 3, width), lambda j: (0, 0, j)),
            pl.BlockSpec((width, k), lambda j: (j, 0)),
        ],
        out_specs=[
            pl.BlockSpec((rows * cols, width), lambda j: (0, j)), fixed(rows * cols), fixed(k),
        ],
        out_shape=[
            jax.ShapeDtypeStruct((total, channels), jnp.bfloat16),
            jax.ShapeDtypeStruct((total, k), jnp.float32),
            jax.ShapeDtypeStruct((k, k), jnp.float32),
        ],
        scratch_shapes=[pltpu.VMEM((2, 10 * (cols + 16), 128), jnp.float32)],
        compiler_params=params(54, 1),
        cost_estimate=pl.CostEstimate(
            flops=2 * rows * cols * channels * (k + 900), transcendentals=0,
            bytes_accessed=4 * rows * cols * channels,
        ),
        name="smooth_sketch",
    )(x, kernel, test_matrix)


def border_body(
    core_ref, upper_ref, lower_ref, c0_ref, c1_ref, c2_ref, c3_ref, top_ref, bot_ref,
    left_ref, right_ref, kern_ref, test_ref, gram_ref, flat_in_ref, sketch_in_ref,
    edge_ref, sketch_ref, keep_ref, send_ref,
):
    step, steps = pl.program_id(0), pl.num_programs(0)
    cols, width = top_ref.shape
    rows = c1_ref.shape[0]
    f32 = jnp.float32
    left, right = left_ref[...].astype(f32), right_ref[...].astype(f32)
    top, bot = top_ref[...].astype(f32), bot_ref[...].astype(f32)
    taps = [[kern_ref[a, b : b + 1, :] for b in range(3)] for a in range(3)]

    def along_row(pixels, lefts, rights):
        total = None
        for a in range(3):
            before = jnp.concatenate([lefts[a], pixels[a][:-1]], axis=0)
            behind = jnp.concatenate([pixels[a][1:], rights[a]], axis=0)
            for b, moved in enumerate((before, pixels[a], behind)):
                term = taps[a][b] * moved
                total = term if total is None else total + term
        return total

    def along_column(columns):
        total = None
        for b in range(3):
            middle, above, below = columns[b]
            up = jnp.concatenate([above, middle[:-1]], axis=0)
            down = jnp.concatenate([middle[1:], below], axis=0)
            for a, moved in enumerate((up, middle, down)):
                term = taps[a][b] * moved
                total = term if total is None else total + term
        place = lax.broadcasted_iota(jnp.int32, total.shape, 0)
        return jnp.where((place == 0) | (place == rows - 1), 0.0, total)

    upper, lower = upper_ref[...].astype(f32), lower_ref[...].astype(f32)
    own = [r[...].astype(f32) for r in (c0_ref, c1_ref, c2_ref, c3_ref)]
    take = lambda v, i: v[i : i + 1]
    first_row = along_row(
        (top, upper[0], upper[1]),
        (take(left, rows), take(left, 0), take(left, 1)),
        (take(right, rows), take(right, 0), take(right, 1)),
    )
    last_row = along_row(
        (lower[0], lower[1], bot),
        (take(left, rows - 2), take(left, rows - 1), take(left, rows + 1)),
        (take(right, rows - 2), take(right, rows - 1), take(right, rows + 1)),
    )
    halo = lambda v: (v[:rows], take(v, rows), take(v, rows + 1))
    ours = lambda i, w: (own[i][:rows], take(top, w), take(bot, w))
    first_column = along_column((halo(left), ours(0, 0), ours(1, 1)))
    last_column = along_column((ours(2, cols - 2), ours(3, cols - 1), halo(right)))
    spare = jnp.zeros((BORDER - 2 * (rows + cols), width), f32)
    edge = jnp.concatenate([first_row, last_row, first_column, last_column, spare], axis=0)
    edge_ref[...] = edge.astype(jnp.bfloat16)
    part = jnp.dot(edge_ref[...], test_ref[...], preferred_element_type=f32)

    @pl.when(step == 0)
    def _():
        sketch_ref[...] = part

    @pl.when(step > 0)
    def _():
        sketch_ref[...] += part

    @pl.when(step == steps - 1)
    def _():
        gram = gram_ref[...] + gram_of(sketch_ref[...])
        half = keep_ref.shape[0]

        @pl.when(core_ref[0] == 0)
        def _():
            keep_ref[...] = gram[:half]
            send_ref[...] = gram[half:]

        @pl.when(core_ref[0] == 1)
        def _():
            keep_ref[...] = gram[half:]
            send_ref[...] = gram[:half]


def border_sketch(core, x, columns, halos, kernel, test_matrix, gram, flat, sketch):
    rows, cols, channels = x.shape
    k = test_matrix.shape[1]
    width = 1024
    edge = lambda n, at=0: pl.BlockSpec((n, width), lambda j, core: (at, j))
    fixed = lambda n, at=0: pl.BlockSpec((n, k), lambda j, core: (at, 0))
    behind = rows * cols // BORDER
    return pl.pallas_call(
        border_body,
        grid_spec=pltpu.PrefetchScalarGridSpec(
            num_scalar_prefetch=1,
            grid=(channels // width,),
            in_specs=[
                pl.BlockSpec((2, cols, width), lambda j, core: (0, 0, j)),
                pl.BlockSpec((2, cols, width), lambda j, core: (rows // 2 - 1, 0, j)),
                edge(rows + 8), edge(rows), edge(rows), edge(rows + 8),
                edge(cols), edge(cols), edge(rows + 8), edge(rows + 8),
                pl.BlockSpec((3, 3, width), lambda j, core: (0, 0, j)),
                pl.BlockSpec((width, k), lambda j, core: (j, 0)),
                fixed(k),
                pl.BlockSpec(memory_space=pl.ANY),
                pl.BlockSpec(memory_space=pl.ANY),
            ],
            out_specs=[edge(BORDER, behind), fixed(BORDER, behind), fixed(k // 2), fixed(k // 2)],
        ),
        out_shape=[
            jax.ShapeDtypeStruct(flat.shape, flat.dtype),
            jax.ShapeDtypeStruct(sketch.shape, sketch.dtype),
            jax.ShapeDtypeStruct((k // 2, k), jnp.float32),
            jax.ShapeDtypeStruct((k // 2, k), jnp.float32),
        ],
        input_output_aliases={14: 0, 15: 1},
        compiler_params=params(52, 1),
        name="border_sketch",
    )(core, x, x, *columns, *halos, kernel, test_matrix, gram, flat, sketch)


def columns_body(low_ref, high_ref, top_ref, bot_ref, c0_ref, c1_ref, c2_ref, c3_ref):
    rows, _, width = low_ref.shape
    cols = top_ref.shape[0]
    f32, bf16 = jnp.float32, jnp.bfloat16
    out_id = lax.broadcasted_iota(jnp.int32, (2 * rows, 8 * rows), 0)
    in_id = lax.broadcasted_iota(jnp.int32, (2 * rows, 8 * rows), 1)
    spare = jnp.zeros((6, width), f32)

    def cut(held_ref, at):
        wanted = (out_id % rows) * 8 + at + out_id // rows
        pick = jnp.where(in_id == wanted, 1.0, 0.0).astype(bf16)
        held = held_ref[...].reshape(8 * rows, width)
        return jnp.dot(pick, held, preferred_element_type=f32)

    def with_ends(column, place):
        ends = [r[...].astype(f32)[place : place + 1] for r in (top_ref, bot_ref)]
        return jnp.concatenate([column] + ends + [spare], axis=0).astype(bf16)

    low, high = cut(low_ref, 0), cut(high_ref, 6)
    c0_ref[...] = with_ends(low[:rows], 0)
    c1_ref[...] = low[rows:].astype(bf16)
    c2_ref[...] = high[:rows].astype(bf16)
    c3_ref[...] = with_ends(high[rows:], cols - 1)


def edge_columns(x, top, bottom):
    rows, cols, channels = x.shape
    width = 1024
    edge = lambda n: pl.BlockSpec((n, width), lambda j: (0, j))
    return pl.pallas_call(
        columns_body,
        grid=(channels // width,),
        in_specs=[
            pl.BlockSpec((rows, 8, width), lambda j: (0, 0, j)),
            pl.BlockSpec((rows, 8, width), lambda j: (0, cols // 8 - 1, j)),
            edge(cols), edge(cols),
        ],
        out_specs=[edge(rows + 8), edge(rows), edge(rows), edge(rows + 8)],
        out_shape=[
            jax.ShapeDtypeStruct((n, channels), x.dtype) for n in (rows + 8, rows, rows, rows + 8)
        ],
        compiler_params=params(52, 1),
        name="edge_columns",
    )(x, x, top, bottom)


def factor_block(panel, low, sub, lane):
    shape = panel.shape
    d = [
        [jnp.broadcast_to(panel[i : i + 1, low + j : low + j + 1], shape) for j in range(i + 1)]
        for i in range(8)
    ]
    e = [[None] * 8 for _ in range(8)]
    for j in range(8):
        scale = lax.rsqrt(d[j][j])
        column = [d[i][j] * scale if i > j else None for i in range(8)]
        for k in range(j):
            e[j][k] = e[j][k] * scale
        e[j][j] = scale
        for i in range(j + 1, 8):
            for k in range(j + 1, i + 1):
                d[i][k] = d[i][k] - column[i] * column[k]
            for k in range(j):
                e[i][k] = e[i][k] - column[i] * e[j][k]
            e[i][j] = -column[i] * scale
    unit = jnp.where(lane == sub + low, 1.0, 0.0)
    panel = jnp.where((lane >= low) & (lane < low + 8), unit, panel)
    total = None
    for k in range(8):
        column = jnp.where(sub == k, e[k][k], 0.0)
        for i in range(k + 1, 8):
            column = jnp.where(sub == i, e[i][k], column)
        term = column * jnp.broadcast_to(panel[k : k + 1, :], shape)
        total = term if total is None else total + term
    return total


def inverse_factor(work_ref):
    n = work_ref.shape[0]
    row_id = lax.broadcasted_iota(jnp.int32, (n, n), 0)
    col_id = lax.broadcasted_iota(jnp.int32, (n, n), 1)
    sub = lax.broadcasted_iota(jnp.int32, (8, n), 0)
    lane = lax.broadcasted_iota(jnp.int32, (8, n), 1)
    panel = work_ref[0:8, :]
    for low in range(0, n, 8):
        near, far = low + 8, low + 16
        done = factor_block(panel, low, sub, lane)
        work_ref[low:near, :] = done
        if far < n:
            update = lax.dot_general(
                done, done, (((0,), (0,)), ((), ())), precision=HIGH,
                preferred_element_type=jnp.float32,
            )
            keep = (col_id[far:] < low) | (col_id[far:] >= near)
            rest = jnp.where(keep, work_ref[far:, :], 0.0) - update[far:, :]
        if near < n:
            turned = done.T[near:far, :]
            panel = jnp.where((lane < low) | (lane >= near), work_ref[near:far, :], 0.0)
            for k in range(8):
                panel = panel - jnp.broadcast_to(turned[:, k : k + 1], panel.shape) * (
                    jnp.broadcast_to(done[k : k + 1, :], panel.shape)
                )
        if far < n:
            work_ref[far:, :] = rest
    return jnp.where(row_id >= col_id, work_ref[...], 0.0)


def times_transposed(values, matrix):
    return lax.dot_general(
        values, matrix, (((1,), (1,)), ((), ())), precision=HIGH,
        preferred_element_type=jnp.float32,
    )


def project_body(
    core_ref, mine_ref, other_ref, sketch_ref, flat_ref, out_ref, work_ref, basis_ref
):
    @pl.when(pl.program_id(0) == 0)
    def _():
        half = mine_ref.shape[0]
        work_ref[pl.ds(pl.multiple_of(core_ref[0] * half, half), half), :] = mine_ref[...]
        work_ref[pl.ds(pl.multiple_of((1 - core_ref[0]) * half, half), half), :] = other_ref[...]
        inverse = inverse_factor(work_ref)
        basis = times_transposed(sketch_ref[...], inverse)
        basis_ref[...] = basis.astype(jnp.bfloat16).T

    product = jnp.dot(basis_ref[...], flat_ref[...], preferred_element_type=jnp.float32)
    out_ref[0] = product.T


def project(core, mine, other, sketch, flat):
    pixels, channels = flat.shape
    k = sketch.shape[1]
    width = 512
    half = channels // width // 2
    whole = lambda *shape: pl.BlockSpec(shape, lambda j, core: (0,) * len(shape))
    return pl.pallas_call(
        project_body,
        grid_spec=pltpu.PrefetchScalarGridSpec(
            num_scalar_prefetch=1,
            grid=(channels // width,),
            in_specs=[
                whole(k // 2, k), whole(k // 2, k), whole(pixels, k),
                pl.BlockSpec((pixels, width), lambda j, core: (0, j)),
            ],
            out_specs=pl.BlockSpec(
                (1, width, k), lambda j, core: ((j // half) ^ core[0], j % half, 0)
            ),
            scratch_shapes=[
                pltpu.VMEM((k, k), jnp.float32), pltpu.VMEM((k, pixels), jnp.bfloat16),
            ],
        ),
        out_shape=jax.ShapeDtypeStruct((2, channels // 2, k), jnp.float32),
        compiler_params=params(40, 1),
        name="project",
    )(core, mine, other, sketch, flat)


def second_body(core_ref, flat_ref, range_ref, second_ref, out_ref, acc_ref):
    step, steps = pl.program_id(0), pl.num_programs(0)
    f32, bf16 = jnp.float32, jnp.bfloat16
    k = range_ref.shape[1]
    values = jnp.dot(flat_ref[...], range_ref[...], preferred_element_type=f32)
    second_ref[...] = values
    high = values.astype(bf16)
    low = (values - high.astype(f32)).astype(bf16)
    both = jnp.concatenate([high, low], axis=1).T

    @pl.when(step == 0)
    def _():
        acc_ref[...] = jnp.dot(both, flat_ref[...], preferred_element_type=f32)

    @pl.when(step > 0)
    def _():
        acc_ref[...] += jnp.dot(both, flat_ref[...], preferred_element_type=f32)

    @pl.when(step == steps - 1)
    def _():
        half = out_ref.shape[1]
        for part in range(2):
            lanes = slice(part * half, part * half + half)
            out_ref[part ^ core_ref[0]] = (acc_ref[:k, lanes] + acc_ref[k:, lanes]).T


def second_step(core, flat, range_map):
    pixels, channels = flat.shape
    k = range_map.shape[1]
    height = 768
    return pl.pallas_call(
        second_body,
        grid_spec=pltpu.PrefetchScalarGridSpec(
            num_scalar_prefetch=1,
            grid=(pixels // height,),
            in_specs=[
                pl.BlockSpec((height, channels), lambda i, core: (i, 0)),
                pl.BlockSpec((channels, k), lambda i, core: (0, 0)),
            ],
            out_specs=[
                pl.BlockSpec((height, k), lambda i, core: (i, 0)),
                pl.BlockSpec((2, channels // 2, k), lambda i, core: (0, 0, 0)),
            ],
            scratch_shapes=[pltpu.VMEM((2 * k, channels), jnp.float32)],
        ),
        out_shape=[
            jax.ShapeDtypeStruct((pixels, k), jnp.float32),
            jax.ShapeDtypeStruct((2, channels // 2, k), jnp.float32),
        ],
        compiler_params=params(48, 1),
        name="second_step",
    )(core, flat, range_map)


def finish_body(
    basis_scale, coeff_scale, range_ref, moment_ref, second_ref,
    basis_ref, coeffs_ref, work_ref,
):
    rows, cols, k = basis_ref.shape
    moment = moment_ref[...]
    work_ref[...] = lax.dot_general(
        range_ref[...].astype(jnp.float32), moment, (((0,), (0,)), ((), ())), precision=HIGH,
        preferred_element_type=jnp.float32,
    )
    inverse = inverse_factor(work_ref)
    basis = times_transposed(second_ref[...], inverse) * basis_scale
    inner = basis[: rows * cols].reshape(rows, cols, k)
    border = basis[rows * cols :]
    place = lax.broadcasted_iota(jnp.int32, inner.shape, 1)
    first = border[2 * cols : 2 * cols + rows].reshape(rows, 1, k)
    last = border[2 * cols + rows : 2 * (cols + rows)].reshape(rows, 1, k)
    basis_ref[...] = jnp.where(place == 0, first, jnp.where(place == cols - 1, last, inner))
    basis_ref[0] = border[:cols]
    basis_ref[rows - 1] = border[cols : 2 * cols]
    coeffs_ref[...] = times_transposed(inverse, moment) * coeff_scale


def finish(range_map, moment, second, tile, basis_scale, coeff_scale):
    channels, k = moment.shape

    def body(*refs):
        finish_body(basis_scale, coeff_scale, *refs)

    return pl.pallas_call(
        body,
        out_shape=[
            jax.ShapeDtypeStruct(tile + (k,), jnp.float32),
            jax.ShapeDtypeStruct((k, channels), jnp.float32),
        ],
        scratch_shapes=[pltpu.VMEM((k, k), jnp.float32)],
        compiler_params=params(40),
        name="finish",
    )(range_map, moment, second)


def all_sum(pair, core, dtype):
    gy, gx = lax.axis_size("gy"), lax.axis_size("gx")
    groups = [[y * gx + x for y in range(c, gy, 2) for x in range(gx)] for c in range(2)]
    half, k = pair.shape[1:]
    members = gy * gx // 2
    swap = lambda v: lax.all_to_all(v, BOTH, 0, 0, axis_index_groups=groups, tiled=True)
    mine = pair[0] + xor_permute(pair[1], "gy", 1)
    parts = swap(mine.reshape(members, half // members, k))
    chunk = jnp.sum(parts, axis=0).astype(dtype)
    chunk = lax.optimization_barrier(chunk)
    whole = swap(jnp.broadcast_to(chunk[None], (members,) + chunk.shape)).reshape(half, k)
    other = xor_permute(whole, "gy", 1)
    first, last = jnp.where(core == 0, whole, other), jnp.where(core == 0, other, whole)
    return jnp.concatenate([first, last], axis=0)


def on_device(radiance, kernel, test_matrix):
    height, breadth, channels = radiance.shape
    devices = lax.axis_size("gy") * lax.axis_size("gx")
    pixel_count = height * breadth * devices
    core = lax.axis_index("gy") % 2
    core_arg = core.astype(jnp.int32).reshape(1)

    top = shift_permute(radiance[-1], "gy", 1)
    bottom = shift_permute(radiance[0], "gy", -1)
    columns = edge_columns(radiance, top, bottom)
    left = shift_permute(columns[3], "gx", 1)
    right = shift_permute(columns[0], "gx", -1)
    halos = (top, bottom, left, right)

    flat, sketch, gram = smooth_sketch(radiance, kernel, test_matrix)
    flat, sketch, mine, send = border_sketch(
        core_arg, radiance, columns, halos, kernel, test_matrix, gram, flat, sketch
    )
    mine = mine + xor_permute(send, "gy", 1)
    for axis, mask in (("gx", 1), ("gx", 3), ("gx", 4), ("gx", 12), ("gy", 2), ("gy", 6)):
        mine = mine + xor_permute(mine, axis, mask)
    other = xor_permute(mine, "gy", 1)
    range_map = all_sum(project(core_arg, mine, other, sketch, flat), core, jnp.bfloat16)
    second, pair = second_step(core_arg, flat, range_map)
    moment = all_sum(pair, core, jnp.float32)
    scale = math.sqrt(pixel_count)
    return finish(
        range_map, moment, second, (height, breadth),
        scale, scale * math.sqrt(channels) / pixel_count,
    )


def solution(mesh):
    placed = (P("gy", "gx", None), P(), P())
    return jax.shard_map(
        on_device, mesh=mesh, in_specs=placed, out_specs=(P("gy", "gx", None), P()), check_vma=False
    )
```

```python
import math

import jax
import jax.numpy as jnp
from jax import lax
from jax.experimental import pallas as pl
from jax.experimental.pallas import tpu as pltpu
from jax.sharding import PartitionSpec as P

HIGH = lax.Precision.HIGHEST
BOTH = ("gy", "gx")
BORDER = 256


def xor_permute(value, axis, mask):
    return lax.ppermute(value, axis, [(i, i ^ mask) for i in range(lax.axis_size(axis))])


def shift_permute(value, axis, step):
    devices = lax.axis_size(axis)
    pairs = [(i, i + step) for i in range(devices) if 0 <= i + step < devices]
    return lax.ppermute(value, axis, pairs)


def params(mib, axes=0):
    return pltpu.CompilerParams(
        vmem_limit_bytes=mib << 20, dimension_semantics=("arbitrary",) * axes if axes else None
    )


def smooth_body(x_ref, kern_ref, test_ref, flat_ref, sketch_ref, gram_ref, pad_ref):
    step, steps = pl.program_id(0), pl.num_programs(0)
    rows, cols, width = x_ref.shape
    f32 = jnp.float32
    group = 8
    groups = rows // group
    sub = lax.broadcasted_iota(jnp.int32, (8, 128), 0)

    @pl.when(step == 0)
    def _():
        sketch_ref[...] = jnp.zeros_like(sketch_ref)

    def project_rows(g):
        span = pl.ds(pl.multiple_of(g * group * cols, group * cols), group * cols)
        return span, jnp.dot(flat_ref[span, :], test_ref[...], preferred_element_type=f32)

    def smooth_rows(g):
        base = pl.multiple_of(g * group, group)
        for chunk in range(width // 128):
            lanes = slice(chunk * 128, chunk * 128 + 128)
            pad = pad_ref.at[chunk % 2]
            taps = [
                [jnp.broadcast_to(kern_ref[a, b : b + 1, lanes], (cols, 128)) for b in range(3)]
                for a in range(3)
            ]

            def fetch(q):
                place = base + q - 1
                if q == 0:
                    place = jnp.maximum(place, 0)
                elif q == group + 1:
                    place = jnp.minimum(place, rows - 1)
                row = x_ref[place, :, lanes].astype(f32)
                at = q * (cols + 16) + 8
                pad[at : at + cols, :] = row
                return [pad[at - 1 : at - 1 + cols, :], row, pad[at + 1 : at + 1 + cols, :]]

            near = [fetch(0), fetch(1)]
            for r in range(group):
                near = near[-2:] + [fetch(r + 2)]
                total = None
                for a in range(3):
                    for b in range(3):
                        term = taps[a][b] * near[a][b]
                        total = term if total is None else total + term
                head = jnp.where(sub == 0, 0.0, total[:8])
                tail = jnp.where(sub == 7, 0.0, total[cols - 8 :])
                total = jnp.concatenate([head, total[8 : cols - 8], tail], axis=0)
                if r == 0:
                    total = jnp.where(g == 0, 0.0, total)
                if r == group - 1:
                    total = jnp.where(g == groups - 1, 0.0, total)
                start = pl.multiple_of((base + r) * cols, cols)
                flat_ref[pl.ds(start, cols), lanes] = total.astype(jnp.bfloat16)

    def body(g, carry):
        span, part = project_rows(g - 1)
        smooth_rows(g)
        sketch_ref[span, :] += part
        return carry

    smooth_rows(0)
    lax.fori_loop(1, groups, body, 0)
    span, part = project_rows(groups - 1)
    sketch_ref[span, :] += part

    @pl.when(step == steps - 1)
    def _():
        gram_ref[...] = gram_of(sketch_ref[...])


def gram_of(values):
    return lax.dot_general(
        values, values, (((0,), (0,)), ((), ())), precision=HIGH,
        preferred_element_type=jnp.float32,
    )


def smooth_sketch(x, kernel, test_matrix):
    rows, cols, channels = x.shape
    k = test_matrix.shape[1]
    width = 512
    total = rows * cols + BORDER
    fixed = lambda n: pl.BlockSpec((n, k), lambda j: (0, 0))
    return pl.pallas_call(
        smooth_body,
        grid=(channels // width,),
        in_specs=[
            pl.BlockSpec((rows, cols, width), lambda j: (0, 0, j)),
            pl.BlockSpec((3, 3, width), lambda j: (0, 0, j)),
            pl.BlockSpec((width, k), lambda j: (j, 0)),
        ],
        out_specs=[
            pl.BlockSpec((rows * cols, width), lambda j: (0, j)), fixed(rows * cols), fixed(k),
        ],
        out_shape=[
            jax.ShapeDtypeStruct((total, channels), jnp.bfloat16),
            jax.ShapeDtypeStruct((total, k), jnp.float32),
            jax.ShapeDtypeStruct((k, k), jnp.float32),
        ],
        scratch_shapes=[pltpu.VMEM((2, 10 * (cols + 16), 128), jnp.float32)],
        compiler_params=params(54, 1),
        cost_estimate=pl.CostEstimate(
            flops=2 * rows * cols * channels * (k + 900), transcendentals=0,
            bytes_accessed=4 * rows * cols * channels,
        ),
        name="smooth_sketch",
    )(x, kernel, test_matrix)


def border_body(
    upper_ref, lower_ref, c0_ref, c1_ref, c2_ref, c3_ref, top_ref, bot_ref,
    left_ref, right_ref, kern_ref, test_ref, gram_ref, flat_in_ref, sketch_in_ref,
    edge_ref, sketch_ref, gram_out_ref,
):
    step, steps = pl.program_id(0), pl.num_programs(0)
    cols, width = top_ref.shape
    rows = c1_ref.shape[0]
    f32 = jnp.float32
    left, right = left_ref[...].astype(f32), right_ref[...].astype(f32)
    top, bot = top_ref[...].astype(f32), bot_ref[...].astype(f32)
    taps = [[kern_ref[a, b : b + 1, :] for b in range(3)] for a in range(3)]

    def along_row(pixels, lefts, rights):
        total = None
        for a in range(3):
            before = jnp.concatenate([lefts[a], pixels[a][:-1]], axis=0)
            behind = jnp.concatenate([pixels[a][1:], rights[a]], axis=0)
            for b, moved in enumerate((before, pixels[a], behind)):
                term = taps[a][b] * moved
                total = term if total is None else total + term
        return total

    def along_column(columns):
        total = None
        for b in range(3):
            middle, above, below = columns[b]
            up = jnp.concatenate([above, middle[:-1]], axis=0)
            down = jnp.concatenate([middle[1:], below], axis=0)
            for a, moved in enumerate((up, middle, down)):
                term = taps[a][b] * moved
                total = term if total is None else total + term
        place = lax.broadcasted_iota(jnp.int32, total.shape, 0)
        return jnp.where((place == 0) | (place == rows - 1), 0.0, total)

    upper, lower = upper_ref[...].astype(f32), lower_ref[...].astype(f32)
    own = [r[...].astype(f32) for r in (c0_ref, c1_ref, c2_ref, c3_ref)]
    take = lambda v, i: v[i : i + 1]
    first_row = along_row(
        (top, upper[0], upper[1]),
        (take(left, rows), take(left, 0), take(left, 1)),
        (take(right, rows), take(right, 0), take(right, 1)),
    )
    last_row = along_row(
        (lower[0], lower[1], bot),
        (take(left, rows - 2), take(left, rows - 1), take(left, rows + 1)),
        (take(right, rows - 2), take(right, rows - 1), take(right, rows + 1)),
    )
    halo = lambda v: (v[:rows], take(v, rows), take(v, rows + 1))
    ours = lambda i, w: (own[i][:rows], take(top, w), take(bot, w))
    first_column = along_column((halo(left), ours(0, 0), ours(1, 1)))
    last_column = along_column((ours(2, cols - 2), ours(3, cols - 1), halo(right)))
    spare = jnp.zeros((BORDER - 2 * (rows + cols), width), f32)
    edge = jnp.concatenate([first_row, last_row, first_column, last_column, spare], axis=0)
    edge_ref[...] = edge.astype(jnp.bfloat16)
    part = jnp.dot(edge_ref[...], test_ref[...], preferred_element_type=f32)

    @pl.when(step == 0)
    def _():
        sketch_ref[...] = part

    @pl.when(step > 0)
    def _():
        sketch_ref[...] += part

    @pl.when(step == steps - 1)
    def _():
        gram_out_ref[...] = gram_ref[...] + gram_of(sketch_ref[...])


def border_sketch(x, columns, halos, kernel, test_matrix, gram, flat, sketch):
    rows, cols, channels = x.shape
    k = test_matrix.shape[1]
    width = 1024
    edge = lambda n, at=0: pl.BlockSpec((n, width), lambda j: (at, j))
    fixed = lambda n, at=0: pl.BlockSpec((n, k), lambda j: (at, 0))
    behind = rows * cols // BORDER
    return pl.pallas_call(
        border_body,
        grid=(channels // width,),
        in_specs=[
            pl.BlockSpec((2, cols, width), lambda j: (0, 0, j)),
            pl.BlockSpec((2, cols, width), lambda j: (rows // 2 - 1, 0, j)),
            edge(rows + 8), edge(rows), edge(rows), edge(rows + 8),
            edge(cols), edge(cols), edge(rows + 8), edge(rows + 8),
            pl.BlockSpec((3, 3, width), lambda j: (0, 0, j)),
            pl.BlockSpec((width, k), lambda j: (j, 0)),
            fixed(k),
            pl.BlockSpec(memory_space=pl.ANY),
            pl.BlockSpec(memory_space=pl.ANY),
        ],
        out_specs=[edge(BORDER, behind), fixed(BORDER, behind), fixed(k)],
        out_shape=[
            jax.ShapeDtypeStruct(flat.shape, flat.dtype),
            jax.ShapeDtypeStruct(sketch.shape, sketch.dtype),
            jax.ShapeDtypeStruct((k, k), jnp.float32),
        ],
        input_output_aliases={13: 0, 14: 1},
        compiler_params=params(52, 1),
        name="border_sketch",
    )(x, x, *columns, *halos, kernel, test_matrix, gram, flat, sketch)


def columns_body(low_ref, high_ref, c0_ref, c1_ref, c2_ref, c3_ref):
    rows, _, width = low_ref.shape
    f32, bf16 = jnp.float32, jnp.bfloat16
    out_id = lax.broadcasted_iota(jnp.int32, (2 * rows, 8 * rows), 0)
    in_id = lax.broadcasted_iota(jnp.int32, (2 * rows, 8 * rows), 1)
    spare = jnp.zeros((8, width), bf16)

    def cut(held_ref, at):
        wanted = (out_id % rows) * 8 + at + out_id // rows
        pick = jnp.where(in_id == wanted, 1.0, 0.0).astype(bf16)
        held = held_ref[...].reshape(8 * rows, width)
        return jnp.dot(pick, held, preferred_element_type=f32).astype(bf16)

    low, high = cut(low_ref, 0), cut(high_ref, 6)
    c0_ref[:rows] = low[:rows]
    c0_ref[rows:] = spare
    c1_ref[...] = low[rows:]
    c2_ref[...] = high[:rows]
    c3_ref[:rows] = high[rows:]
    c3_ref[rows:] = spare


def edge_columns(x):
    rows, cols, channels = x.shape
    width = 1024
    edge = lambda n: pl.BlockSpec((n, width), lambda j: (0, j))
    return pl.pallas_call(
        columns_body,
        grid=(channels // width,),
        in_specs=[
            pl.BlockSpec((rows, 8, width), lambda j: (0, 0, j)),
            pl.BlockSpec((rows, 8, width), lambda j: (0, cols // 8 - 1, j)),
        ],
        out_specs=[edge(rows + 8), edge(rows), edge(rows), edge(rows + 8)],
        out_shape=[
            jax.ShapeDtypeStruct((n, channels), x.dtype) for n in (rows + 8, rows, rows, rows + 8)
        ],
        compiler_params=params(52, 1),
        cost_estimate=pl.CostEstimate(
            flops=2 * 4 * rows * 8 * rows * channels, transcendentals=0,
            bytes_accessed=2 * 20 * rows * channels,
        ),
        name="edge_columns",
    )(x, x)


def factor_block(panel, low, sub, lane):
    shape = panel.shape
    d = [
        [jnp.broadcast_to(panel[i : i + 1, low + j : low + j + 1], shape) for j in range(i + 1)]
        for i in range(8)
    ]
    e = [[None] * 8 for _ in range(8)]
    for j in range(8):
        scale = lax.rsqrt(d[j][j])
        column = [d[i][j] * scale if i > j else None for i in range(8)]
        for k in range(j):
            e[j][k] = e[j][k] * scale
        e[j][j] = scale
        for i in range(j + 1, 8):
            for k in range(j + 1, i + 1):
                d[i][k] = d[i][k] - column[i] * column[k]
            for k in range(j):
                e[i][k] = e[i][k] - column[i] * e[j][k]
            e[i][j] = -column[i] * scale
    unit = jnp.where(lane == sub + low, 1.0, 0.0)
    panel = jnp.where((lane >= low) & (lane < low + 8), unit, panel)
    total = None
    for k in range(8):
        column = jnp.where(sub == k, e[k][k], 0.0)
        for i in range(k + 1, 8):
            column = jnp.where(sub == i, e[i][k], column)
        term = column * jnp.broadcast_to(panel[k : k + 1, :], shape)
        total = term if total is None else total + term
    return total


def inverse_factor(work_ref):
    n = work_ref.shape[0]
    row_id = lax.broadcasted_iota(jnp.int32, (n, n), 0)
    col_id = lax.broadcasted_iota(jnp.int32, (n, n), 1)
    sub = lax.broadcasted_iota(jnp.int32, (8, n), 0)
    lane = lax.broadcasted_iota(jnp.int32, (8, n), 1)
    panel = work_ref[0:8, :]
    for low in range(0, n, 8):
        near, far = low + 8, low + 16
        done = factor_block(panel, low, sub, lane)
        work_ref[low:near, :] = done
        if far < n:
            update = lax.dot_general(
                done, done, (((0,), (0,)), ((), ())), precision=HIGH,
                preferred_element_type=jnp.float32,
            )
            keep = (col_id[far:] < low) | (col_id[far:] >= near)
            rest = jnp.where(keep, work_ref[far:, :], 0.0) - update[far:, :]
        if near < n:
            turned = done.T[near:far, :]
            panel = jnp.where((lane < low) | (lane >= near), work_ref[near:far, :], 0.0)
            for k in range(8):
                panel = panel - jnp.broadcast_to(turned[:, k : k + 1], panel.shape) * (
                    jnp.broadcast_to(done[k : k + 1, :], panel.shape)
                )
        if far < n:
            work_ref[far:, :] = rest
    return jnp.where(row_id >= col_id, work_ref[...], 0.0)


def times_transposed(values, matrix):
    return lax.dot_general(
        values, matrix, (((1,), (1,)), ((), ())), precision=HIGH,
        preferred_element_type=jnp.float32,
    )


def project_body(
    core_ref, gram_ref, sketch_ref, flat_ref, out_ref, work_ref, basis_ref
):
    @pl.when(pl.program_id(0) == 0)
    def _():
        work_ref[...] = gram_ref[...]
        inverse = inverse_factor(work_ref)
        basis = times_transposed(sketch_ref[...], inverse)
        basis_ref[...] = basis.astype(jnp.bfloat16).T

    product = jnp.dot(basis_ref[...], flat_ref[...], preferred_element_type=jnp.float32)
    out_ref[0] = product.T


def project(core, gram, sketch, flat):
    pixels, channels = flat.shape
    k = sketch.shape[1]
    width = 512
    half = channels // width // 2
    whole = lambda *shape: pl.BlockSpec(shape, lambda j, core: (0,) * len(shape))
    return pl.pallas_call(
        project_body,
        grid_spec=pltpu.PrefetchScalarGridSpec(
            num_scalar_prefetch=1,
            grid=(channels // width,),
            in_specs=[
                whole(k, k), whole(pixels, k),
                pl.BlockSpec((pixels, width), lambda j, core: (0, j)),
            ],
            out_specs=pl.BlockSpec(
                (1, width, k), lambda j, core: ((j // half) ^ core[0], j % half, 0)
            ),
            scratch_shapes=[
                pltpu.VMEM((k, k), jnp.float32), pltpu.VMEM((k, pixels), jnp.bfloat16),
            ],
        ),
        out_shape=jax.ShapeDtypeStruct((2, channels // 2, k), jnp.float32),
        compiler_params=params(40, 1),
        name="project",
    )(core, gram, sketch, flat)


def second_body(core_ref, flat_ref, range_ref, second_ref, out_ref, acc_ref):
    step, steps = pl.program_id(0), pl.num_programs(0)
    f32, bf16 = jnp.float32, jnp.bfloat16
    k = range_ref.shape[1]
    values = jnp.dot(flat_ref[...], range_ref[...], preferred_element_type=f32)
    second_ref[...] = values
    high = values.astype(bf16)
    low = (values - high.astype(f32)).astype(bf16)
    both = jnp.concatenate([high, low], axis=1).T

    @pl.when(step == 0)
    def _():
        acc_ref[...] = jnp.dot(both, flat_ref[...], preferred_element_type=f32)

    @pl.when(step > 0)
    def _():
        acc_ref[...] += jnp.dot(both, flat_ref[...], preferred_element_type=f32)

    @pl.when(step == steps - 1)
    def _():
        half = out_ref.shape[1]
        for part in range(2):
            lanes = slice(part * half, part * half + half)
            out_ref[part ^ core_ref[0]] = (acc_ref[:k, lanes] + acc_ref[k:, lanes]).T


def second_step(core, flat, range_map):
    pixels, channels = flat.shape
    k = range_map.shape[1]
    height = 768
    return pl.pallas_call(
        second_body,
        grid_spec=pltpu.PrefetchScalarGridSpec(
            num_scalar_prefetch=1,
            grid=(pixels // height,),
            in_specs=[
                pl.BlockSpec((height, channels), lambda i, core: (i, 0)),
                pl.BlockSpec((channels, k), lambda i, core: (0, 0)),
            ],
            out_specs=[
                pl.BlockSpec((height, k), lambda i, core: (i, 0)),
                pl.BlockSpec((2, channels // 2, k), lambda i, core: (0, 0, 0)),
            ],
            scratch_shapes=[pltpu.VMEM((2 * k, channels), jnp.float32)],
        ),
        out_shape=[
            jax.ShapeDtypeStruct((pixels, k), jnp.float32),
            jax.ShapeDtypeStruct((2, channels // 2, k), jnp.float32),
        ],
        compiler_params=params(48, 1),
        name="second_step",
    )(core, flat, range_map)


def finish_body(
    basis_scale, coeff_scale, range_ref, moment_ref, second_ref,
    basis_ref, coeffs_ref, work_ref,
):
    rows, cols, k = basis_ref.shape
    moment = moment_ref[...]
    work_ref[...] = lax.dot_general(
        range_ref[...].astype(jnp.float32), moment, (((0,), (0,)), ((), ())), precision=HIGH,
        preferred_element_type=jnp.float32,
    )
    inverse = inverse_factor(work_ref)
    basis = times_transposed(second_ref[...], inverse) * basis_scale
    inner = basis[: rows * cols].reshape(rows, cols, k)
    border = basis[rows * cols :]
    place = lax.broadcasted_iota(jnp.int32, inner.shape, 1)
    first = border[2 * cols : 2 * cols + rows].reshape(rows, 1, k)
    last = border[2 * cols + rows : 2 * (cols + rows)].reshape(rows, 1, k)
    basis_ref[...] = jnp.where(place == 0, first, jnp.where(place == cols - 1, last, inner))
    basis_ref[0] = border[:cols]
    basis_ref[rows - 1] = border[cols : 2 * cols]
    coeffs_ref[...] = times_transposed(inverse, moment) * coeff_scale


def finish(range_map, moment, second, tile, basis_scale, coeff_scale):
    channels, k = moment.shape

    def body(*refs):
        finish_body(basis_scale, coeff_scale, *refs)

    return pl.pallas_call(
        body,
        out_shape=[
            jax.ShapeDtypeStruct(tile + (k,), jnp.float32),
            jax.ShapeDtypeStruct((k, channels), jnp.float32),
        ],
        scratch_shapes=[pltpu.VMEM((k, k), jnp.float32)],
        compiler_params=params(40),
        name="finish",
    )(range_map, moment, second)


def all_sum(pair, core, dtype):
    gy, gx = lax.axis_size("gy"), lax.axis_size("gx")
    groups = [[y * gx + x for y in range(c, gy, 2) for x in range(gx)] for c in range(2)]
    half, k = pair.shape[1:]
    members = gy * gx // 2
    swap = lambda v: lax.all_to_all(v, BOTH, 0, 0, axis_index_groups=groups, tiled=True)
    mine = pair[0] + xor_permute(pair[1], "gy", 1)
    parts = swap(mine.reshape(members, half // members, k))
    chunk = jnp.sum(parts, axis=0).astype(dtype)
    chunk = lax.optimization_barrier(chunk)
    whole = swap(jnp.broadcast_to(chunk[None], (members,) + chunk.shape)).reshape(half, k)
    other = xor_permute(whole, "gy", 1)
    first, last = jnp.where(core == 0, whole, other), jnp.where(core == 0, other, whole)
    return jnp.concatenate([first, last], axis=0)


def on_device(radiance, kernel, test_matrix):
    height, breadth, channels = radiance.shape
    devices = lax.axis_size("gy") * lax.axis_size("gx")
    pixel_count = height * breadth * devices
    core = lax.axis_index("gy") % 2
    core_arg = core.astype(jnp.int32).reshape(1)

    top = shift_permute(radiance[-1], "gy", 1)
    bottom = shift_permute(radiance[0], "gy", -1)
    first, second, before_last, last = edge_columns(radiance)
    first = lax.dynamic_update_slice(first, jnp.stack([top[0], bottom[0]]), (height, 0))
    last = lax.dynamic_update_slice(last, jnp.stack([top[-1], bottom[-1]]), (height, 0))
    columns = (first, second, before_last, last)
    left = shift_permute(last, "gx", 1)
    right = shift_permute(first, "gx", -1)
    halos = (top, bottom, left, right)

    flat, sketch, gram = smooth_sketch(radiance, kernel, test_matrix)
    flat, sketch, gram = border_sketch(
        radiance, columns, halos, kernel, test_matrix, gram, flat, sketch
    )
    gram = gram + xor_permute(gram, "gy", 1)
    for axis, masks in (("gx", (1, 2, 3)), ("gx", (4, 8, 12)), ("gy", (2, 4, 6))):
        one, two, three = [xor_permute(gram, axis, mask) for mask in masks]
        gram = (gram + one) + (two + three)
    range_map = all_sum(project(core_arg, gram, sketch, flat), core, jnp.bfloat16)
    second, pair = second_step(core_arg, flat, range_map)
    moment = all_sum(pair, core, jnp.float32)
    scale = math.sqrt(pixel_count)
    return finish(
        range_map, moment, second, (height, breadth),
        scale, scale * math.sqrt(channels) / pixel_count,
    )


def solution(mesh):
    placed = (P("gy", "gx", None), P(), P())
    return jax.shard_map(
        on_device, mesh=mesh, in_specs=placed, out_specs=(P("gy", "gx", None), P()), check_vma=False
    )
```

```python
import math

import jax
import jax.numpy as jnp
from jax import lax
from jax.experimental import pallas as pl
from jax.experimental.pallas import tpu as pltpu
from jax.sharding import PartitionSpec as P

HIGH = lax.Precision.HIGHEST
BOTH = ("gy", "gx")
BORDER = 256


def xor_permute(value, axis, mask):
    return lax.ppermute(value, axis, [(i, i ^ mask) for i in range(lax.axis_size(axis))])


def shift_permute(value, axis, step):
    devices = lax.axis_size(axis)
    pairs = [(i, i + step) for i in range(devices) if 0 <= i + step < devices]
    return lax.ppermute(value, axis, pairs)


def params(mib, axes=0):
    return pltpu.CompilerParams(
        vmem_limit_bytes=mib << 20, dimension_semantics=("arbitrary",) * axes if axes else None
    )


def smooth_body(x_ref, kern_ref, test_ref, flat_ref, sketch_ref, gram_ref, pad_ref):
    step, steps = pl.program_id(0), pl.num_programs(0)
    rows, cols, width = x_ref.shape
    f32 = jnp.float32
    group = 8
    groups = rows // group
    sub = lax.broadcasted_iota(jnp.int32, (8, 128), 0)

    @pl.when(step == 0)
    def _():
        sketch_ref[...] = jnp.zeros_like(sketch_ref)

    def project_rows(g):
        span = pl.ds(pl.multiple_of(g * group * cols, group * cols), group * cols)
        return span, jnp.dot(flat_ref[span, :], test_ref[...], preferred_element_type=f32)

    def smooth_rows(g, first=0, last=0):
        base = pl.multiple_of(g * group, group)
        for chunk in range(width // 128):
            lanes = slice(chunk * 128, chunk * 128 + 128)
            pad = pad_ref.at[chunk % 2]
            taps = [
                [jnp.broadcast_to(kern_ref[a, b : b + 1, lanes], (cols, 128)) for b in range(3)]
                for a in range(3)
            ]

            def fetch(q):
                row = x_ref[base + q - 1, :, lanes].astype(f32)
                at = q * (cols + 16) + 8
                pad[at : at + cols, :] = row
                return [pad[at - 1 : at - 1 + cols, :], row, pad[at + 1 : at + 1 + cols, :]]

            near = [fetch(q) for q in (first, first + 1)]
            for r in range(first, group - last):
                near = near[-2:] + [fetch(r + 2)]
                total = None
                for a in range(3):
                    for b in range(3):
                        term = taps[a][b] * near[a][b]
                        total = term if total is None else total + term
                head = jnp.where(sub == 0, 0.0, total[:8])
                tail = jnp.where(sub == 7, 0.0, total[cols - 8 :])
                total = jnp.concatenate([head, total[8 : cols - 8], tail], axis=0)
                start = pl.multiple_of((base + r) * cols, cols)
                flat_ref[pl.ds(start, cols), lanes] = total.astype(jnp.bfloat16)

    def body(g, carry):
        span, part = project_rows(g - 1)
        smooth_rows(g)
        sketch_ref[span, :] += part
        return carry

    flat_ref[:cols, :] = jnp.zeros((cols, width), jnp.bfloat16)
    flat_ref[(rows - 1) * cols :, :] = jnp.zeros((cols, width), jnp.bfloat16)
    smooth_rows(0, first=1)
    lax.fori_loop(1, groups - 1, body, 0)
    span, part = project_rows(groups - 2)
    smooth_rows(groups - 1, last=1)
    sketch_ref[span, :] += part
    span, part = project_rows(groups - 1)
    sketch_ref[span, :] += part

    @pl.when(step == steps - 1)
    def _():
        gram_ref[...] = gram_of(sketch_ref[...])


def gram_of(values):
    return lax.dot_general(
        values, values, (((0,), (0,)), ((), ())), precision=HIGH,
        preferred_element_type=jnp.float32,
    )


def smooth_sketch(x, kernel, test_matrix):
    rows, cols, channels = x.shape
    k = test_matrix.shape[1]
    width = 512
    total = rows * cols + BORDER
    fixed = lambda n: pl.BlockSpec((n, k), lambda j: (0, 0))
    return pl.pallas_call(
        smooth_body,
        grid=(channels // width,),
        in_specs=[
            pl.BlockSpec((rows, cols, width), lambda j: (0, 0, j)),
            pl.BlockSpec((3, 3, width), lambda j: (0, 0, j)),
            pl.BlockSpec((width, k), lambda j: (j, 0)),
        ],
        out_specs=[
            pl.BlockSpec((rows * cols, width), lambda j: (0, j)), fixed(rows * cols), fixed(k),
        ],
        out_shape=[
            jax.ShapeDtypeStruct((total, channels), jnp.bfloat16),
            jax.ShapeDtypeStruct((total, k), jnp.float32),
            jax.ShapeDtypeStruct((k, k), jnp.float32),
        ],
        scratch_shapes=[pltpu.VMEM((2, 10 * (cols + 16), 128), jnp.float32)],
        compiler_params=params(54, 1),
        cost_estimate=pl.CostEstimate(
            flops=2 * rows * cols * channels * (k + 900), transcendentals=0,
            bytes_accessed=4 * rows * cols * channels,
        ),
        name="smooth_sketch",
    )(x, kernel, test_matrix)


def border_body(
    upper_ref, lower_ref, c0_ref, c1_ref, c2_ref, c3_ref, top_ref, bot_ref,
    left_ref, right_ref, kern_ref, test_ref, gram_ref, flat_in_ref, sketch_in_ref,
    edge_ref, sketch_ref, gram_out_ref,
):
    step, steps = pl.program_id(0), pl.num_programs(0)
    cols, width = top_ref.shape
    rows = c1_ref.shape[0]
    f32 = jnp.float32
    left, right = left_ref[...].astype(f32), right_ref[...].astype(f32)
    top, bot = top_ref[...].astype(f32), bot_ref[...].astype(f32)
    taps = [[kern_ref[a, b : b + 1, :] for b in range(3)] for a in range(3)]

    def along_row(pixels, lefts, rights):
        total = None
        for a in range(3):
            before = jnp.concatenate([lefts[a], pixels[a][:-1]], axis=0)
            behind = jnp.concatenate([pixels[a][1:], rights[a]], axis=0)
            for b, moved in enumerate((before, pixels[a], behind)):
                term = taps[a][b] * moved
                total = term if total is None else total + term
        return total

    def along_column(columns):
        total = None
        for b in range(3):
            middle, above, below = columns[b]
            up = jnp.concatenate([above, middle[:-1]], axis=0)
            down = jnp.concatenate([middle[1:], below], axis=0)
            for a, moved in enumerate((up, middle, down)):
                term = taps[a][b] * moved
                total = term if total is None else total + term
        place = lax.broadcasted_iota(jnp.int32, total.shape, 0)
        return jnp.where((place == 0) | (place == rows - 1), 0.0, total)

    upper, lower = upper_ref[...].astype(f32), lower_ref[...].astype(f32)
    own = [r[...].astype(f32) for r in (c0_ref, c1_ref, c2_ref, c3_ref)]
    take = lambda v, i: v[i : i + 1]
    first_row = along_row(
        (top, upper[0], upper[1]),
        (take(left, rows), take(left, 0), take(left, 1)),
        (take(right, rows), take(right, 0), take(right, 1)),
    )
    last_row = along_row(
        (lower[0], lower[1], bot),
        (take(left, rows - 2), take(left, rows - 1), take(left, rows + 1)),
        (take(right, rows - 2), take(right, rows - 1), take(right, rows + 1)),
    )
    halo = lambda v: (v[:rows], take(v, rows), take(v, rows + 1))
    ours = lambda i, w: (own[i][:rows], take(top, w), take(bot, w))
    first_column = along_column((halo(left), ours(0, 0), ours(1, 1)))
    last_column = along_column((ours(2, cols - 2), ours(3, cols - 1), halo(right)))
    spare = jnp.zeros((BORDER - 2 * (rows + cols), width), f32)
    edge = jnp.concatenate([first_row, last_row, first_column, last_column, spare], axis=0)
    edge_ref[...] = edge.astype(jnp.bfloat16)
    part = jnp.dot(edge_ref[...], test_ref[...], preferred_element_type=f32)

    @pl.when(step == 0)
    def _():
        sketch_ref[...] = part

    @pl.when(step > 0)
    def _():
        sketch_ref[...] += part

    @pl.when(step == steps - 1)
    def _():
        gram_out_ref[...] = gram_ref[...] + gram_of(sketch_ref[...])


def border_sketch(x, columns, halos, kernel, test_matrix, gram, flat, sketch):
    rows, cols, channels = x.shape
    k = test_matrix.shape[1]
    width = 1024
    edge = lambda n, at=0: pl.BlockSpec((n, width), lambda j: (at, j))
    fixed = lambda n, at=0: pl.BlockSpec((n, k), lambda j: (at, 0))
    behind = rows * cols // BORDER
    return pl.pallas_call(
        border_body,
        grid=(channels // width,),
        in_specs=[
            pl.BlockSpec((2, cols, width), lambda j: (0, 0, j)),
            pl.BlockSpec((2, cols, width), lambda j: (rows // 2 - 1, 0, j)),
            edge(rows + 8), edge(rows), edge(rows), edge(rows + 8),
            edge(cols), edge(cols), edge(rows + 8), edge(rows + 8),
            pl.BlockSpec((3, 3, width), lambda j: (0, 0, j)),
            pl.BlockSpec((width, k), lambda j: (j, 0)),
            fixed(k),
            pl.BlockSpec(memory_space=pl.ANY),
            pl.BlockSpec(memory_space=pl.ANY),
        ],
        out_specs=[edge(BORDER, behind), fixed(BORDER, behind), fixed(k)],
        out_shape=[
            jax.ShapeDtypeStruct(flat.shape, flat.dtype),
            jax.ShapeDtypeStruct(sketch.shape, sketch.dtype),
            jax.ShapeDtypeStruct((k, k), jnp.float32),
        ],
        input_output_aliases={13: 0, 14: 1},
        compiler_params=params(52, 1),
        name="border_sketch",
    )(x, x, *columns, *halos, kernel, test_matrix, gram, flat, sketch)


def columns_body(low_ref, high_ref, c0_ref, c1_ref, c2_ref, c3_ref):
    rows, _, width = low_ref.shape
    f32, bf16 = jnp.float32, jnp.bfloat16
    out_id = lax.broadcasted_iota(jnp.int32, (2 * rows, 8 * rows), 0)
    in_id = lax.broadcasted_iota(jnp.int32, (2 * rows, 8 * rows), 1)
    spare = jnp.zeros((8, width), bf16)

    def cut(held_ref, at):
        wanted = (out_id % rows) * 8 + at + out_id // rows
        pick = jnp.where(in_id == wanted, 1.0, 0.0).astype(bf16)
        held = held_ref[...].reshape(8 * rows, width)
        return jnp.dot(pick, held, preferred_element_type=f32).astype(bf16)

    low, high = cut(low_ref, 0), cut(high_ref, 6)
    c0_ref[:rows] = low[:rows]
    c0_ref[rows:] = spare
    c1_ref[...] = low[rows:]
    c2_ref[...] = high[:rows]
    c3_ref[:rows] = high[rows:]
    c3_ref[rows:] = spare


def edge_columns(x):
    rows, cols, channels = x.shape
    width = 2048
    edge = lambda n: pl.BlockSpec((n, width), lambda j: (0, j))
    return pl.pallas_call(
        columns_body,
        grid=(channels // width,),
        in_specs=[
            pl.BlockSpec((rows, 8, width), lambda j: (0, 0, j)),
            pl.BlockSpec((rows, 8, width), lambda j: (0, cols // 8 - 1, j)),
        ],
        out_specs=[edge(rows + 8), edge(rows), edge(rows), edge(rows + 8)],
        out_shape=[
            jax.ShapeDtypeStruct((n, channels), x.dtype) for n in (rows + 8, rows, rows, rows + 8)
        ],
        compiler_params=params(52, 1),
        cost_estimate=pl.CostEstimate(
            flops=2 * 4 * rows * 8 * rows * channels, transcendentals=0,
            bytes_accessed=2 * 20 * rows * channels,
        ),
        name="edge_columns",
    )(x, x)


def factor_block(panel, low, sub, lane):
    shape = panel.shape
    d = [
        [jnp.broadcast_to(panel[i : i + 1, low + j : low + j + 1], shape) for j in range(i + 1)]
        for i in range(8)
    ]
    e = [[None] * 8 for _ in range(8)]
    for j in range(8):
        scale = lax.rsqrt(d[j][j])
        column = [d[i][j] * scale if i > j else None for i in range(8)]
        for k in range(j):
            e[j][k] = e[j][k] * scale
        e[j][j] = scale
        for i in range(j + 1, 8):
            for k in range(j + 1, i + 1):
                d[i][k] = d[i][k] - column[i] * column[k]
            for k in range(j):
                e[i][k] = e[i][k] - column[i] * e[j][k]
            e[i][j] = -column[i] * scale
    unit = jnp.where(lane == sub + low, 1.0, 0.0)
    panel = jnp.where((lane >= low) & (lane < low + 8), unit, panel)
    total = None
    for k in range(8):
        column = jnp.where(sub == k, e[k][k], 0.0)
        for i in range(k + 1, 8):
            column = jnp.where(sub == i, e[i][k], column)
        term = column * jnp.broadcast_to(panel[k : k + 1, :], shape)
        total = term if total is None else total + term
    return total


def inverse_factor(work_ref):
    n = work_ref.shape[0]
    row_id = lax.broadcasted_iota(jnp.int32, (n, n), 0)
    col_id = lax.broadcasted_iota(jnp.int32, (n, n), 1)
    sub = lax.broadcasted_iota(jnp.int32, (8, n), 0)
    lane = lax.broadcasted_iota(jnp.int32, (8, n), 1)
    panel = work_ref[0:8, :]
    for low in range(0, n, 8):
        near, far = low + 8, low + 16
        done = factor_block(panel, low, sub, lane)
        work_ref[low:near, :] = done
        if far < n:
            update = lax.dot_general(
                done, done, (((0,), (0,)), ((), ())), precision=HIGH,
                preferred_element_type=jnp.float32,
            )
            keep = (col_id[far:] < low) | (col_id[far:] >= near)
            rest = jnp.where(keep, work_ref[far:, :], 0.0) - update[far:, :]
        if near < n:
            turned = done.T[near:far, :]
            panel = jnp.where((lane < low) | (lane >= near), work_ref[near:far, :], 0.0)
            for k in range(8):
                panel = panel - jnp.broadcast_to(turned[:, k : k + 1], panel.shape) * (
                    jnp.broadcast_to(done[k : k + 1, :], panel.shape)
                )
        if far < n:
            work_ref[far:, :] = rest
    return jnp.where(row_id >= col_id, work_ref[...], 0.0)


def times_transposed(values, matrix):
    return lax.dot_general(
        values, matrix, (((1,), (1,)), ((), ())), precision=HIGH,
        preferred_element_type=jnp.float32,
    )


def project_other_body(core_ref, gram_ref, sketch_ref, flat_ref, out_ref, basis_ref, work_ref):
    @pl.when(pl.program_id(0) == 0)
    def _():
        work_ref[...] = gram_ref[...]
        inverse = inverse_factor(work_ref)
        basis = times_transposed(sketch_ref[...], inverse)
        basis_ref[...] = basis.astype(jnp.bfloat16).T

    product = jnp.dot(basis_ref[...], flat_ref[...], preferred_element_type=jnp.float32)
    out_ref[...] = product.T


def project_own_body(core_ref, basis_ref, flat_ref, out_ref):
    product = jnp.dot(basis_ref[...], flat_ref[...], preferred_element_type=jnp.float32)
    out_ref[...] = product.T


def project_other(core, gram, sketch, flat):
    pixels, channels = flat.shape
    k = sketch.shape[1]
    width = 512
    half = channels // width // 2
    whole = lambda *shape: pl.BlockSpec(shape, lambda j, core: (0,) * len(shape))
    return pl.pallas_call(
        project_other_body,
        grid_spec=pltpu.PrefetchScalarGridSpec(
            num_scalar_prefetch=1,
            grid=(half,),
            in_specs=[
                whole(k, k), whole(pixels, k),
                pl.BlockSpec((pixels, width), lambda j, core: (0, (1 - core[0]) * half + j)),
            ],
            out_specs=[pl.BlockSpec((width, k), lambda j, core: (j, 0)), whole(k, pixels)],
            scratch_shapes=[pltpu.VMEM((k, k), jnp.float32)],
        ),
        out_shape=[
            jax.ShapeDtypeStruct((channels // 2, k), jnp.float32),
            jax.ShapeDtypeStruct((k, pixels), jnp.bfloat16),
        ],
        compiler_params=params(40, 1),
        name="project_other",
    )(core, gram, sketch, flat)


def project_own(core, basis, flat):
    pixels, channels = flat.shape
    k = basis.shape[0]
    width = 512
    half = channels // width // 2
    return pl.pallas_call(
        project_own_body,
        grid_spec=pltpu.PrefetchScalarGridSpec(
            num_scalar_prefetch=1,
            grid=(half,),
            in_specs=[
                pl.BlockSpec((k, pixels), lambda j, core: (0, 0)),
                pl.BlockSpec((pixels, width), lambda j, core: (0, core[0] * half + j)),
            ],
            out_specs=pl.BlockSpec((width, k), lambda j, core: (j, 0)),
        ),
        out_shape=jax.ShapeDtypeStruct((channels // 2, k), jnp.float32),
        compiler_params=params(40, 1),
        cost_estimate=pl.CostEstimate(
            flops=4 * pixels * channels * k, transcendentals=0, bytes_accessed=pixels * channels
        ),
        name="project_own",
    )(core, basis, flat)


def second_body(core_ref, flat_ref, range_ref, second_ref, out_ref, acc_ref):
    step, steps = pl.program_id(0), pl.num_programs(0)
    f32, bf16 = jnp.float32, jnp.bfloat16
    k = range_ref.shape[1]
    values = jnp.dot(flat_ref[...], range_ref[...], preferred_element_type=f32)
    second_ref[...] = values
    high = values.astype(bf16)
    low = (values - high.astype(f32)).astype(bf16)
    both = jnp.concatenate([high, low], axis=1).T

    @pl.when(step == 0)
    def _():
        acc_ref[...] = jnp.dot(both, flat_ref[...], preferred_element_type=f32)

    @pl.when(step > 0)
    def _():
        acc_ref[...] += jnp.dot(both, flat_ref[...], preferred_element_type=f32)

    @pl.when(step == steps - 1)
    def _():
        half = out_ref.shape[1]
        for part in range(2):
            lanes = slice(part * half, part * half + half)
            out_ref[part ^ core_ref[0]] = (acc_ref[:k, lanes] + acc_ref[k:, lanes]).T


def second_step(core, flat, range_map):
    pixels, channels = flat.shape
    k = range_map.shape[1]
    height = 768
    return pl.pallas_call(
        second_body,
        grid_spec=pltpu.PrefetchScalarGridSpec(
            num_scalar_prefetch=1,
            grid=(pixels // height,),
            in_specs=[
                pl.BlockSpec((height, channels), lambda i, core: (i, 0)),
                pl.BlockSpec((channels, k), lambda i, core: (0, 0)),
            ],
            out_specs=[
                pl.BlockSpec((height, k), lambda i, core: (i, 0)),
                pl.BlockSpec((2, channels // 2, k), lambda i, core: (0, 0, 0)),
            ],
            scratch_shapes=[pltpu.VMEM((2 * k, channels), jnp.float32)],
        ),
        out_shape=[
            jax.ShapeDtypeStruct((pixels, k), jnp.float32),
            jax.ShapeDtypeStruct((2, channels // 2, k), jnp.float32),
        ],
        compiler_params=params(48, 1),
        name="second_step",
    )(core, flat, range_map)


def finish_body(
    basis_scale, coeff_scale, range_ref, moment_ref, second_ref,
    basis_ref, coeffs_ref, work_ref,
):
    rows, cols, k = basis_ref.shape
    moment = moment_ref[...]
    work_ref[...] = lax.dot_general(
        range_ref[...].astype(jnp.float32), moment, (((0,), (0,)), ((), ())), precision=HIGH,
        preferred_element_type=jnp.float32,
    )
    inverse = inverse_factor(work_ref)
    basis = times_transposed(second_ref[...], inverse) * basis_scale
    inner = basis[: rows * cols].reshape(rows, cols, k)
    border = basis[rows * cols :]
    place = lax.broadcasted_iota(jnp.int32, inner.shape, 1)
    first = border[2 * cols : 2 * cols + rows].reshape(rows, 1, k)
    last = border[2 * cols + rows : 2 * (cols + rows)].reshape(rows, 1, k)
    basis_ref[...] = jnp.where(place == 0, first, jnp.where(place == cols - 1, last, inner))
    basis_ref[0] = border[:cols]
    basis_ref[rows - 1] = border[cols : 2 * cols]
    coeffs_ref[...] = times_transposed(inverse, moment) * coeff_scale


def finish(range_map, moment, second, tile, basis_scale, coeff_scale):
    channels, k = moment.shape

    def body(*refs):
        finish_body(basis_scale, coeff_scale, *refs)

    return pl.pallas_call(
        body,
        out_shape=[
            jax.ShapeDtypeStruct(tile + (k,), jnp.float32),
            jax.ShapeDtypeStruct((k, channels), jnp.float32),
        ],
        scratch_shapes=[pltpu.VMEM((k, k), jnp.float32)],
        compiler_params=params(40),
        name="finish",
    )(range_map, moment, second)


def all_sum(own, received, core, dtype):
    gy, gx = lax.axis_size("gy"), lax.axis_size("gx")
    groups = [[y * gx + x for y in range(c, gy, 2) for x in range(gx)] for c in range(2)]
    half, k = own.shape
    members = gy * gx // 2
    swap = lambda v: lax.all_to_all(v, BOTH, 0, 0, axis_index_groups=groups, tiled=True)
    mine = own + received
    parts = swap(mine.reshape(members, half // members, k))
    chunk = jnp.sum(parts, axis=0).astype(dtype)
    chunk = lax.optimization_barrier(chunk)
    whole = swap(jnp.broadcast_to(chunk[None], (members,) + chunk.shape)).reshape(half, k)
    other = xor_permute(whole, "gy", 1)
    first, last = jnp.where(core == 0, whole, other), jnp.where(core == 0, other, whole)
    return jnp.concatenate([first, last], axis=0)


def on_device(radiance, kernel, test_matrix):
    height, breadth, channels = radiance.shape
    devices = lax.axis_size("gy") * lax.axis_size("gx")
    pixel_count = height * breadth * devices
    core = lax.axis_index("gy") % 2
    core_arg = core.astype(jnp.int32).reshape(1)

    top = shift_permute(radiance[-1], "gy", 1)
    bottom = shift_permute(radiance[0], "gy", -1)
    first, second, before_last, last = edge_columns(radiance)
    first = lax.dynamic_update_slice(first, jnp.stack([top[0], bottom[0]]), (height, 0))
    last = lax.dynamic_update_slice(last, jnp.stack([top[-1], bottom[-1]]), (height, 0))
    columns = (first, second, before_last, last)
    left = shift_permute(last, "gx", 1)
    right = shift_permute(first, "gx", -1)
    halos = (top, bottom, left, right)

    flat, sketch, gram = smooth_sketch(radiance, kernel, test_matrix)
    flat, sketch, gram = border_sketch(
        radiance, columns, halos, kernel, test_matrix, gram, flat, sketch
    )
    gram = gram + xor_permute(gram, "gy", 1)
    for axis, masks in (("gx", (1, 2, 3)), ("gx", (4, 8, 12)), ("gy", (2, 4, 6))):
        one, two, three = [xor_permute(gram, axis, mask) for mask in masks]
        gram = (gram + one) + (two + three)
    part, basis = project_other(core_arg, gram, sketch, flat)
    received = xor_permute(part, "gy", 1)
    range_map = all_sum(project_own(core_arg, basis, flat), received, core, jnp.bfloat16)
    second, pair = second_step(core_arg, flat, range_map)
    moment = all_sum(pair[0], xor_permute(pair[1], "gy", 1), core, jnp.float32)
    scale = math.sqrt(pixel_count)
    return finish(
        range_map, moment, second, (height, breadth),
        scale, scale * math.sqrt(channels) / pixel_count,
    )


def solution(mesh):
    placed = (P("gy", "gx", None), P(), P())
    return jax.shard_map(
        on_device, mesh=mesh, in_specs=placed, out_specs=(P("gy", "gx", None), P()), check_vma=False
    )
```

```python
import math

import jax
import jax.numpy as jnp
from jax import lax
from jax.experimental import pallas as pl
from jax.experimental.pallas import tpu as pltpu
from jax.sharding import PartitionSpec as P

HIGH = lax.Precision.HIGHEST
BOTH = ("gy", "gx")
BORDER = 256


def xor_permute(value, axis, mask):
    return lax.ppermute(value, axis, [(i, i ^ mask) for i in range(lax.axis_size(axis))])


def shift_permute(value, axis, step):
    devices = lax.axis_size(axis)
    pairs = [(i, i + step) for i in range(devices) if 0 <= i + step < devices]
    return lax.ppermute(value, axis, pairs)


def params(mib, axes=0):
    return pltpu.CompilerParams(
        vmem_limit_bytes=mib << 20, dimension_semantics=("arbitrary",) * axes if axes else None
    )


def smooth_body(x_ref, kern_ref, test_ref, flat_ref, sketch_ref, gram_ref, pad_ref):
    step, steps = pl.program_id(0), pl.num_programs(0)
    rows, cols, width = x_ref.shape
    f32 = jnp.float32
    group = 8
    groups = rows // group
    sub = lax.broadcasted_iota(jnp.int32, (8, 128), 0)

    @pl.when(step == 0)
    def _():
        sketch_ref[...] = jnp.zeros_like(sketch_ref)

    def project_rows(g):
        span = pl.ds(pl.multiple_of(g * group * cols, group * cols), group * cols)
        return span, jnp.dot(flat_ref[span, :], test_ref[...], preferred_element_type=f32)

    def smooth_rows(g, first=0, last=0):
        base = pl.multiple_of(g * group, group)
        for chunk in range(width // 128):
            lanes = slice(chunk * 128, chunk * 128 + 128)
            pad = pad_ref.at[chunk % 2]
            taps = [
                [jnp.broadcast_to(kern_ref[a, b : b + 1, lanes], (cols, 128)) for b in range(3)]
                for a in range(3)
            ]

            def fetch(q):
                row = x_ref[base + q - 1, :, lanes].astype(f32)
                at = q * (cols + 16) + 8
                pad[at : at + cols, :] = row
                return [pad[at - 1 : at - 1 + cols, :], row, pad[at + 1 : at + 1 + cols, :]]

            near = [fetch(q) for q in (first, first + 1)]
            for r in range(first, group - last):
                near = near[-2:] + [fetch(r + 2)]
                total = None
                for a in range(3):
                    for b in range(3):
                        term = taps[a][b] * near[a][b]
                        total = term if total is None else total + term
                head = jnp.where(sub == 0, 0.0, total[:8])
                tail = jnp.where(sub == 7, 0.0, total[cols - 8 :])
                total = jnp.concatenate([head, total[8 : cols - 8], tail], axis=0)
                start = pl.multiple_of((base + r) * cols, cols)
                flat_ref[pl.ds(start, cols), lanes] = total.astype(jnp.bfloat16)

    def body(g, carry):
        span, part = project_rows(g - 1)
        smooth_rows(g)
        sketch_ref[span, :] += part
        return carry

    flat_ref[:cols, :] = jnp.zeros((cols, width), jnp.bfloat16)
    flat_ref[(rows - 1) * cols :, :] = jnp.zeros((cols, width), jnp.bfloat16)
    smooth_rows(0, first=1)
    lax.fori_loop(1, groups - 1, body, 0)
    span, part = project_rows(groups - 2)
    smooth_rows(groups - 1, last=1)
    sketch_ref[span, :] += part
    span, part = project_rows(groups - 1)
    sketch_ref[span, :] += part

    @pl.when(step == steps - 1)
    def _():
        gram_ref[...] = gram_of(sketch_ref[...])


def gram_of(values):
    return lax.dot_general(
        values, values, (((0,), (0,)), ((), ())), precision=HIGH,
        preferred_element_type=jnp.float32,
    )


def smooth_sketch(x, kernel, test_matrix):
    rows, cols, channels = x.shape
    k = test_matrix.shape[1]
    width = 512
    total = rows * cols + BORDER
    fixed = lambda n: pl.BlockSpec((n, k), lambda j: (0, 0))
    return pl.pallas_call(
        smooth_body,
        grid=(channels // width,),
        in_specs=[
            pl.BlockSpec((rows, cols, width), lambda j: (0, 0, j)),
            pl.BlockSpec((3, 3, width), lambda j: (0, 0, j)),
            pl.BlockSpec((width, k), lambda j: (j, 0)),
        ],
        out_specs=[
            pl.BlockSpec((rows * cols, width), lambda j: (0, j)), fixed(rows * cols), fixed(k),
        ],
        out_shape=[
            jax.ShapeDtypeStruct((total, channels), jnp.bfloat16),
            jax.ShapeDtypeStruct((total, k), jnp.float32),
            jax.ShapeDtypeStruct((k, k), jnp.float32),
        ],
        scratch_shapes=[pltpu.VMEM((2, 10 * (cols + 16), 128), jnp.float32)],
        compiler_params=params(54, 1),
        cost_estimate=pl.CostEstimate(
            flops=2 * rows * cols * channels * (k + 900), transcendentals=0,
            bytes_accessed=4 * rows * cols * channels,
        ),
        name="smooth_sketch",
    )(x, kernel, test_matrix)


def border_body(
    upper_ref, lower_ref, c0_ref, c1_ref, c2_ref, c3_ref, top_ref, bot_ref,
    left_ref, right_ref, kern_ref, test_ref, gram_ref, flat_in_ref, sketch_in_ref,
    edge_ref, sketch_ref, gram_out_ref,
):
    step, steps = pl.program_id(0), pl.num_programs(0)
    cols, width = top_ref.shape
    rows = c1_ref.shape[0]
    f32 = jnp.float32
    left, right = left_ref[...].astype(f32), right_ref[...].astype(f32)
    top, bot = top_ref[...].astype(f32), bot_ref[...].astype(f32)
    taps = [[kern_ref[a, b : b + 1, :] for b in range(3)] for a in range(3)]

    def along_row(pixels, lefts, rights):
        total = None
        for a in range(3):
            before = jnp.concatenate([lefts[a], pixels[a][:-1]], axis=0)
            behind = jnp.concatenate([pixels[a][1:], rights[a]], axis=0)
            for b, moved in enumerate((before, pixels[a], behind)):
                term = taps[a][b] * moved
                total = term if total is None else total + term
        return total

    def along_column(columns):
        total = None
        for b in range(3):
            middle, above, below = columns[b]
            up = jnp.concatenate([above, middle[:-1]], axis=0)
            down = jnp.concatenate([middle[1:], below], axis=0)
            for a, moved in enumerate((up, middle, down)):
                term = taps[a][b] * moved
                total = term if total is None else total + term
        place = lax.broadcasted_iota(jnp.int32, total.shape, 0)
        return jnp.where((place == 0) | (place == rows - 1), 0.0, total)

    upper, lower = upper_ref[...].astype(f32), lower_ref[...].astype(f32)
    own = [r[...].astype(f32) for r in (c0_ref, c1_ref, c2_ref, c3_ref)]
    take = lambda v, i: v[i : i + 1]
    first_row = along_row(
        (top, upper[0], upper[1]),
        (take(left, rows), take(left, 0), take(left, 1)),
        (take(right, rows), take(right, 0), take(right, 1)),
    )
    last_row = along_row(
        (lower[0], lower[1], bot),
        (take(left, rows - 2), take(left, rows - 1), take(left, rows + 1)),
        (take(right, rows - 2), take(right, rows - 1), take(right, rows + 1)),
    )
    halo = lambda v: (v[:rows], take(v, rows), take(v, rows + 1))
    ours = lambda i, w: (own[i][:rows], take(top, w), take(bot, w))
    first_column = along_column((halo(left), ours(0, 0), ours(1, 1)))
    last_column = along_column((ours(2, cols - 2), ours(3, cols - 1), halo(right)))
    spare = jnp.zeros((BORDER - 2 * (rows + cols), width), f32)
    edge = jnp.concatenate([first_row, last_row, first_column, last_column, spare], axis=0)
    edge_ref[...] = edge.astype(jnp.bfloat16)
    part = jnp.dot(edge_ref[...], test_ref[...], preferred_element_type=f32)

    @pl.when(step == 0)
    def _():
        sketch_ref[...] = part

    @pl.when(step > 0)
    def _():
        sketch_ref[...] += part

    @pl.when(step == steps - 1)
    def _():
        gram_out_ref[...] = gram_ref[...] + gram_of(sketch_ref[...])


def border_sketch(x, columns, halos, kernel, test_matrix, gram, flat, sketch):
    rows, cols, channels = x.shape
    k = test_matrix.shape[1]
    width = 1024
    edge = lambda n, at=0: pl.BlockSpec((n, width), lambda j: (at, j))
    fixed = lambda n, at=0: pl.BlockSpec((n, k), lambda j: (at, 0))
    behind = rows * cols // BORDER
    return pl.pallas_call(
        border_body,
        grid=(channels // width,),
        in_specs=[
            pl.BlockSpec((2, cols, width), lambda j: (0, 0, j)),
            pl.BlockSpec((2, cols, width), lambda j: (rows // 2 - 1, 0, j)),
            edge(rows + 8), edge(rows), edge(rows), edge(rows + 8),
            edge(cols), edge(cols), edge(rows + 8), edge(rows + 8),
            pl.BlockSpec((3, 3, width), lambda j: (0, 0, j)),
            pl.BlockSpec((width, k), lambda j: (j, 0)),
            fixed(k),
            pl.BlockSpec(memory_space=pl.ANY),
            pl.BlockSpec(memory_space=pl.ANY),
        ],
        out_specs=[edge(BORDER, behind), fixed(BORDER, behind), fixed(k)],
        out_shape=[
            jax.ShapeDtypeStruct(flat.shape, flat.dtype),
            jax.ShapeDtypeStruct(sketch.shape, sketch.dtype),
            jax.ShapeDtypeStruct((k, k), jnp.float32),
        ],
        input_output_aliases={13: 0, 14: 1},
        compiler_params=params(52, 1),
        name="border_sketch",
    )(x, x, *columns, *halos, kernel, test_matrix, gram, flat, sketch)


def columns_body(low_ref, high_ref, c0_ref, c1_ref, c2_ref, c3_ref):
    rows, _, width = low_ref.shape
    f32, bf16 = jnp.float32, jnp.bfloat16
    out_id = lax.broadcasted_iota(jnp.int32, (2 * rows, 8 * rows), 0)
    in_id = lax.broadcasted_iota(jnp.int32, (2 * rows, 8 * rows), 1)
    spare = jnp.zeros((8, width), bf16)

    def cut(held_ref, at):
        wanted = (out_id % rows) * 8 + at + out_id // rows
        pick = jnp.where(in_id == wanted, 1.0, 0.0).astype(bf16)
        held = held_ref[...].reshape(8 * rows, width)
        return jnp.dot(pick, held, preferred_element_type=f32).astype(bf16)

    low, high = cut(low_ref, 0), cut(high_ref, 6)
    c0_ref[:rows] = low[:rows]
    c0_ref[rows:] = spare
    c1_ref[...] = low[rows:]
    c2_ref[...] = high[:rows]
    c3_ref[:rows] = high[rows:]
    c3_ref[rows:] = spare


def edge_columns(x):
    rows, cols, channels = x.shape
    width = 2048
    edge = lambda n: pl.BlockSpec((n, width), lambda j: (0, j))
    return pl.pallas_call(
        columns_body,
        grid=(channels // width,),
        in_specs=[
            pl.BlockSpec((rows, 8, width), lambda j: (0, 0, j)),
            pl.BlockSpec((rows, 8, width), lambda j: (0, cols // 8 - 1, j)),
        ],
        out_specs=[edge(rows + 8), edge(rows), edge(rows), edge(rows + 8)],
        out_shape=[
            jax.ShapeDtypeStruct((n, channels), x.dtype) for n in (rows + 8, rows, rows, rows + 8)
        ],
        compiler_params=params(52, 1),
        cost_estimate=pl.CostEstimate(
            flops=2 * 4 * rows * 8 * rows * channels, transcendentals=0,
            bytes_accessed=2 * 20 * rows * channels,
        ),
        name="edge_columns",
    )(x, x)


def factor_block(panel, low, sub, lane):
    shape = panel.shape
    d = [
        [jnp.broadcast_to(panel[i : i + 1, low + j : low + j + 1], shape) for j in range(i + 1)]
        for i in range(8)
    ]
    e = [[None] * 8 for _ in range(8)]
    for j in range(8):
        scale = lax.rsqrt(d[j][j])
        column = [d[i][j] * scale if i > j else None for i in range(8)]
        for k in range(j):
            e[j][k] = e[j][k] * scale
        e[j][j] = scale
        for i in range(j + 1, 8):
            for k in range(j + 1, i + 1):
                d[i][k] = d[i][k] - column[i] * column[k]
            for k in range(j):
                e[i][k] = e[i][k] - column[i] * e[j][k]
            e[i][j] = -column[i] * scale
    unit = jnp.where(lane == sub + low, 1.0, 0.0)
    panel = jnp.where((lane >= low) & (lane < low + 8), unit, panel)
    total = None
    for k in range(8):
        column = jnp.where(sub == k, e[k][k], 0.0)
        for i in range(k + 1, 8):
            column = jnp.where(sub == i, e[i][k], column)
        term = column * jnp.broadcast_to(panel[k : k + 1, :], shape)
        total = term if total is None else total + term
    return total


def inverse_factor(work_ref):
    n = work_ref.shape[0]
    row_id = lax.broadcasted_iota(jnp.int32, (n, n), 0)
    col_id = lax.broadcasted_iota(jnp.int32, (n, n), 1)
    sub = lax.broadcasted_iota(jnp.int32, (8, n), 0)
    lane = lax.broadcasted_iota(jnp.int32, (8, n), 1)
    panel = work_ref[0:8, :]
    for low in range(0, n, 8):
        near, far = low + 8, low + 16
        done = factor_block(panel, low, sub, lane)
        work_ref[low:near, :] = done
        if far < n:
            update = lax.dot_general(
                done, done, (((0,), (0,)), ((), ())), precision=HIGH,
                preferred_element_type=jnp.float32,
            )
            keep = (col_id[far:] < low) | (col_id[far:] >= near)
            rest = jnp.where(keep, work_ref[far:, :], 0.0) - update[far:, :]
        if near < n:
            turned = done.T[near:far, :]
            panel = jnp.where((lane < low) | (lane >= near), work_ref[near:far, :], 0.0)
            for k in range(8):
                panel = panel - jnp.broadcast_to(turned[:, k : k + 1], panel.shape) * (
                    jnp.broadcast_to(done[k : k + 1, :], panel.shape)
                )
        if far < n:
            work_ref[far:, :] = rest
    return jnp.where(row_id >= col_id, work_ref[...], 0.0)


def times_transposed(values, matrix):
    return lax.dot_general(
        values, matrix, (((1,), (1,)), ((), ())), precision=HIGH,
        preferred_element_type=jnp.float32,
    )


def project_other_body(core_ref, gram_ref, sketch_ref, flat_ref, out_ref, basis_ref, work_ref):
    @pl.when(pl.program_id(0) == 0)
    def _():
        work_ref[...] = gram_ref[...]
        inverse = inverse_factor(work_ref)
        basis = times_transposed(sketch_ref[...], inverse)
        basis_ref[...] = basis.astype(jnp.bfloat16).T

    product = jnp.dot(basis_ref[...], flat_ref[...], preferred_element_type=jnp.float32)
    out_ref[...] = product.T


def project_own_body(core_ref, basis_ref, flat_ref, out_ref):
    product = jnp.dot(basis_ref[...], flat_ref[...], preferred_element_type=jnp.float32)
    out_ref[...] = product.T


def project_other(core, gram, sketch, flat):
    pixels, channels = flat.shape
    k = sketch.shape[1]
    width = 512
    half = channels // width // 2
    whole = lambda *shape: pl.BlockSpec(shape, lambda j, core: (0,) * len(shape))
    return pl.pallas_call(
        project_other_body,
        grid_spec=pltpu.PrefetchScalarGridSpec(
            num_scalar_prefetch=1,
            grid=(half,),
            in_specs=[
                whole(k, k), whole(pixels, k),
                pl.BlockSpec((pixels, width), lambda j, core: (0, (1 - core[0]) * half + j)),
            ],
            out_specs=[pl.BlockSpec((width, k), lambda j, core: (j, 0)), whole(k, pixels)],
            scratch_shapes=[pltpu.VMEM((k, k), jnp.float32)],
        ),
        out_shape=[
            jax.ShapeDtypeStruct((channels // 2, k), jnp.float32),
            jax.ShapeDtypeStruct((k, pixels), jnp.bfloat16),
        ],
        compiler_params=params(40, 1),
        name="project_other",
    )(core, gram, sketch, flat)


def project_own(core, basis, flat):
    pixels, channels = flat.shape
    k = basis.shape[0]
    width = 512
    half = channels // width // 2
    return pl.pallas_call(
        project_own_body,
        grid_spec=pltpu.PrefetchScalarGridSpec(
            num_scalar_prefetch=1,
            grid=(half,),
            in_specs=[
                pl.BlockSpec((k, pixels), lambda j, core: (0, 0)),
                pl.BlockSpec((pixels, width), lambda j, core: (0, core[0] * half + j)),
            ],
            out_specs=pl.BlockSpec((width, k), lambda j, core: (j, 0)),
        ),
        out_shape=jax.ShapeDtypeStruct((channels // 2, k), jnp.float32),
        compiler_params=params(40, 1),
        cost_estimate=pl.CostEstimate(
            flops=4 * pixels * channels * k, transcendentals=0, bytes_accessed=pixels * channels
        ),
        name="project_own",
    )(core, basis, flat)


def second_body(core_ref, flat_ref, range_ref, second_ref, out_ref, acc_ref):
    step, steps = pl.program_id(0), pl.num_programs(0)
    f32, bf16 = jnp.float32, jnp.bfloat16
    k = range_ref.shape[1]
    values = jnp.dot(flat_ref[...], range_ref[...], preferred_element_type=f32)
    second_ref[...] = values
    high = values.astype(bf16)
    low = (values - high.astype(f32)).astype(bf16)
    both = jnp.concatenate([high, low], axis=1).T

    @pl.when(step == 0)
    def _():
        acc_ref[...] = jnp.dot(both, flat_ref[...], preferred_element_type=f32)

    @pl.when(step > 0)
    def _():
        acc_ref[...] += jnp.dot(both, flat_ref[...], preferred_element_type=f32)

    @pl.when(step == steps - 1)
    def _():
        half = out_ref.shape[1]
        for part in range(2):
            lanes = slice(part * half, part * half + half)
            out_ref[part ^ core_ref[0]] = (acc_ref[:k, lanes] + acc_ref[k:, lanes]).T


def second_step(core, flat, range_map):
    pixels, channels = flat.shape
    k = range_map.shape[1]
    height = 768
    return pl.pallas_call(
        second_body,
        grid_spec=pltpu.PrefetchScalarGridSpec(
            num_scalar_prefetch=1,
            grid=(pixels // height,),
            in_specs=[
                pl.BlockSpec((height, channels), lambda i, core: (i, 0)),
                pl.BlockSpec((channels, k), lambda i, core: (0, 0)),
            ],
            out_specs=[
                pl.BlockSpec((height, k), lambda i, core: (i, 0)),
                pl.BlockSpec((2, channels // 2, k), lambda i, core: (0, 0, 0)),
            ],
            scratch_shapes=[pltpu.VMEM((2 * k, channels), jnp.float32)],
        ),
        out_shape=[
            jax.ShapeDtypeStruct((pixels, k), jnp.float32),
            jax.ShapeDtypeStruct((2, channels // 2, k), jnp.float32),
        ],
        compiler_params=params(48, 1),
        name="second_step",
    )(core, flat, range_map)


def finish_body(
    basis_scale, coeff_scale, range_ref, moment_ref, second_ref,
    basis_ref, coeffs_ref, work_ref,
):
    rows, cols, k = basis_ref.shape
    moment = moment_ref[...]
    terms, left = [], moment
    for _ in range(3):
        terms.append(left.astype(jnp.bfloat16))
        left = left - terms[-1].astype(jnp.float32)
    gram = lax.dot_general(
        range_ref[...], jnp.concatenate(terms, axis=1), (((0,), (0,)), ((), ())),
        preferred_element_type=jnp.float32,
    )
    work_ref[...] = gram[:, :k] + (gram[:, k : 2 * k] + gram[:, 2 * k :])
    inverse = inverse_factor(work_ref)
    basis = times_transposed(second_ref[...], inverse) * basis_scale
    inner = basis[: rows * cols].reshape(rows, cols, k)
    border = basis[rows * cols :]
    place = lax.broadcasted_iota(jnp.int32, inner.shape, 1)
    first = border[2 * cols : 2 * cols + rows].reshape(rows, 1, k)
    last = border[2 * cols + rows : 2 * (cols + rows)].reshape(rows, 1, k)
    basis_ref[...] = jnp.where(place == 0, first, jnp.where(place == cols - 1, last, inner))
    basis_ref[0] = border[:cols]
    basis_ref[rows - 1] = border[cols : 2 * cols]
    coeffs_ref[...] = times_transposed(inverse, moment) * coeff_scale


def finish(range_map, moment, second, tile, basis_scale, coeff_scale):
    channels, k = moment.shape

    def body(*refs):
        finish_body(basis_scale, coeff_scale, *refs)

    return pl.pallas_call(
        body,
        out_shape=[
            jax.ShapeDtypeStruct(tile + (k,), jnp.float32),
            jax.ShapeDtypeStruct((k, channels), jnp.float32),
        ],
        scratch_shapes=[pltpu.VMEM((k, k), jnp.float32)],
        compiler_params=params(40),
        name="finish",
    )(range_map, moment, second)


def all_sum(own, received, core, dtype):
    gy, gx = lax.axis_size("gy"), lax.axis_size("gx")
    groups = [[y * gx + x for y in range(c, gy, 2) for x in range(gx)] for c in range(2)]
    half, k = own.shape
    members = gy * gx // 2
    swap = lambda v: lax.all_to_all(v, BOTH, 0, 0, axis_index_groups=groups, tiled=True)
    mine = own + received
    parts = swap(mine.reshape(members, half // members, k))
    chunk = jnp.sum(parts, axis=0).astype(dtype)
    chunk = lax.optimization_barrier(chunk)
    whole = swap(jnp.broadcast_to(chunk[None], (members,) + chunk.shape)).reshape(half, k)
    other = xor_permute(whole, "gy", 1)
    first, last = jnp.where(core == 0, whole, other), jnp.where(core == 0, other, whole)
    return jnp.concatenate([first, last], axis=0)


def on_device(radiance, kernel, test_matrix):
    height, breadth, channels = radiance.shape
    devices = lax.axis_size("gy") * lax.axis_size("gx")
    pixel_count = height * breadth * devices
    core = lax.axis_index("gy") % 2
    core_arg = core.astype(jnp.int32).reshape(1)

    top = shift_permute(radiance[-1], "gy", 1)
    bottom = shift_permute(radiance[0], "gy", -1)
    first, second, before_last, last = edge_columns(radiance)
    first = lax.dynamic_update_slice(first, jnp.stack([top[0], bottom[0]]), (height, 0))
    last = lax.dynamic_update_slice(last, jnp.stack([top[-1], bottom[-1]]), (height, 0))
    columns = (first, second, before_last, last)
    left = shift_permute(last, "gx", 1)
    right = shift_permute(first, "gx", -1)
    halos = (top, bottom, left, right)

    flat, sketch, gram = smooth_sketch(radiance, kernel, test_matrix)
    flat, sketch, gram = border_sketch(
        radiance, columns, halos, kernel, test_matrix, gram, flat, sketch
    )
    gram = gram + xor_permute(gram, "gy", 1)
    for axis, masks in (("gx", (1, 2, 3)), ("gx", (4, 8, 12)), ("gy", (2, 4, 6))):
        one, two, three = [xor_permute(gram, axis, mask) for mask in masks]
        gram = (gram + one) + (two + three)
    part, basis = project_other(core_arg, gram, sketch, flat)
    received = xor_permute(part, "gy", 1)
    range_map = all_sum(project_own(core_arg, basis, flat), received, core, jnp.bfloat16)
    second, pair = second_step(core_arg, flat, range_map)
    moment = all_sum(pair[0], xor_permute(pair[1], "gy", 1), core, jnp.float32)
    scale = math.sqrt(pixel_count)
    return finish(
        range_map, moment, second, (height, breadth),
        scale, scale * math.sqrt(channels) / pixel_count,
    )


def solution(mesh):
    placed = (P("gy", "gx", None), P(), P())
    return jax.shard_map(
        on_device, mesh=mesh, in_specs=placed, out_specs=(P("gy", "gx", None), P()), check_vma=False
    )
```
